32 devices in a mesh: expert: 8 (over z, x), shard: 4 (over y, core).
Axes of the slice: x: 2, y: 2, z: 4, core: 2. Of those that a mesh axis runs over, the one named last changes fastest.
Arguments:
- tokens: bfloat16 [8192, 2048], P(('expert', 'shard')), may hold values from -6 to 6
- out_grad: bfloat16 [8192, 2048], P(('expert', 'shard')), may hold values from -6 to 6
- routes: int32 [8192, 8], P(('expert', 'shard')), may hold values from 0 to 15, as said below
- segments: int32 [8192], P('expert'), may hold values from 0 to 31, never falling along the last dimension, each value on 1 to 1024 neighbouring positions
- capacity: int32 [16], replicated, may hold values from 64 to 128, as said below
- attn_gain: bfloat16 [2048], P('shard'), may hold values from 0.5 to 1.5
- w_qkv: bfloat16 [2048, 6144], P('shard'), may hold values from -0.125 to 0.125
- query_gain: bfloat16 [128], P('shard'), may hold values from 0.5 to 1.5
- key_gain: bfloat16 [128], P('shard'), may hold values from 0.5 to 1.5
- w_out: bfloat16 [2048, 2048], P('shard'), may hold values from -0.5 to 0.5
- ffn_gain: bfloat16 [2048], P('shard'), may hold values from 0.5 to 1.5
- w_router: bfloat16 [2048, 16], P('shard'), may hold values from -0.0625 to 0.0625
- w_gate_up: bfloat16 [16, 2, 2048, 1024], P('expert', None, None, 'shard'), may hold values from -0.125 to 0.125
- w_down: bfloat16 [16, 1024, 2048], P('expert', 'shard'), may hold values from -6 to 6
Outputs:
- layer_out: bfloat16 [8192, 2048], P(('expert', 'shard'))
- tokens_grad: float32 [8192, 2048], P(('expert', 'shard'))
- attn_gain_grad: float32 [2048], P('shard')
- w_qkv_grad: float32 [2048, 6144], P('shard')
- query_gain_grad: float32 [128], P('shard')
- key_gain_grad: float32 [128], P('shard')
- w_out_grad: float32 [2048, 2048], P('shard')
- ffn_gain_grad: float32 [2048], P('shard')
- w_router_grad: float32 [2048, 16], P('shard')
- w_gate_up_grad: float32 [16, 2, 2048, 1024], P('expert', None, None, 'shard')
- w_down_grad: float32 [16, 1024, 2048], P('expert', 'shard')
The draws below stay inside these ranges and needn't reach their ends.
Inputs may be any that keep to these rules, and one draw needn't show every extreme that they name: `routes`: each token names 8 different experts. `capacity`: some expert has 128 slots. `segments`: document numbers never fall along the tokens.
All inputs are finite; a program needn't handle non-finite values.
Results may differ from the reference program's by a relative error of at most 0.025.
Values may be sent and summed in bfloat16 or wider, within the bound.
No kernel may reach another device: no remote copies, remote signals or barrier semaphores. Data moves between devices by JAX's collectives and lax.ppermute only.
A program may use at most 512 MiB of HBM per device.

```python
import math
import jax
import jax.numpy as jnp
import numpy as np
from jax import lax

D = 2048
HEADS = 16
HEAD_DIM = 128
EXPERT_FF = 1024
TOPK = 8
TOK_DEV = 256
EXPERTS = 16
SEQ_LEN = 1024
TOKENS = 8192
CAP = 128
DOCS = 32
N_EXPERT = 8
N_SHARD = 4


def routing_tables(key):
    popular_key = jax.random.fold_in(key, 101)
    noise_key = jax.random.fold_in(key, 102)
    limit_key = jax.random.fold_in(key, 103)
    popular = jax.random.randint(popular_key, (EXPERTS,), 0, 3 << 18, dtype=jnp.int32)
    noise_draw = jax.random.randint(noise_key, (TOKENS, EXPERTS), 0, 1 << 20, dtype=jnp.int32)
    expert_ids = jnp.arange(EXPERTS, dtype=jnp.int32)
    scores = (noise_draw + popular[None, :]) * EXPERTS + expert_ids[None, :]
    unused, chosen = lax.top_k(scores, TOPK)
    leader = lax.top_k(popular * EXPERTS + expert_ids, 1)[1][0]
    limits = jax.random.randint(limit_key, (EXPERTS,), CAP // 2, CAP + 1, dtype=jnp.int32)
    limits = limits.at[leader].set(CAP)
    limits = limits.at[(leader + 1) % EXPERTS].set(CAP // 2)
    return (chosen.astype(jnp.int32), limits.astype(jnp.int32))


def draw_routes(key, part):
    return routing_tables(key)[0]


def draw_capacity(key, part):
    return routing_tables(key)[1]


def shard_levels(rng, dims, shards, least, high):
    def one(dim, shards_of):
        draws = jax.random.uniform(jax.random.fold_in(jax.random.fold_in(rng, 6), dim), (shards_of,), jnp.float32, least / len(shards), high / len(shards))
        return jnp.repeat(jnp.exp(draws), dims[dim] // shards_of).reshape((-1,) + (1,) * (len(dims) - dim - 1))

    level = one(*shards[0])
    for cut in shards[1:]:
        level = level * one(*cut)
    return level


def length_profile(count, total, reach, skew):
    loads = [(1 << 20) // math.isqrt(standing ** skew) + 1 for standing in range(2, count + 1)]
    surplus, counts = total - reach - (count - 1), [1] * (count - 1)
    while surplus > 0:
        free = [i for i in range(count - 1) if counts[i] < reach]
        pool, left = sum([loads[i] for i in free]), surplus
        for i in free:
            extra = min(reach - counts[i], max(1, left * loads[i] // pool), surplus)
            counts[i] = counts[i] + extra
            surplus = surplus - extra
    return np.array([reach] + counts)


def uneven_parts(own_key, count, total, most, skew):
    if count == 2:
        one = jax.random.randint(own_key, (), max(1, total - most), min(most, total - 1) + 1)
        return jnp.stack([one, total - one])
    sizes = jnp.asarray(length_profile(count, total, most, skew), jnp.int32)
    couples = (count - 1) // 2
    donor, sink = sizes[1:1 + 2 * couples:2], sizes[2:2 + 2 * couples:2]
    margin = jnp.minimum(donor - 1, most - sink)
    passed = jax.random.randint(jax.random.fold_in(own_key, 1), (couples,), 0, 1 << 20) % (margin + 1)
    sizes = sizes.at[1:1 + 2 * couples:2].set(donor - passed).at[2:2 + 2 * couples:2].set(sink + passed)
    return sizes[jax.random.permutation(jax.random.fold_in(own_key, 2), count)]


def bell_draw(rng, shape, scale, most, cuts=(), kind=jnp.bfloat16):
    values = scale * jax.random.normal(rng, shape, jnp.float32)
    if cuts:
        values = values * shard_levels(rng, shape, cuts, -0.22, 0.18)
    return jnp.clip(values, -most, most).astype(kind)


def setup_inputs(seed: int = 0) -> dict:
    key_list = jax.random.split(jax.random.key(seed), 15)
    return {
        "tokens": bell_draw(key_list[0], (TOKENS, D), 1.0, 6.0, ((0, 32),)),
        "out_grad": bell_draw(key_list[1], (TOKENS, D), 1.0, 6.0, ((0, 32),)),
        "routes": draw_routes(jax.random.fold_in(key_list[14], 71), 0),
        "segments": jnp.searchsorted(jnp.cumsum(uneven_parts(key_list[3], DOCS, TOKENS, SEQ_LEN, 2)), jnp.arange(TOKENS), side="right").astype(jnp.int32),
        "capacity": draw_capacity(jax.random.fold_in(key_list[14], 71), 0),
        "attn_gain": jnp.clip(1.0 + 0.1 * jax.random.normal(key_list[5], (D,), jnp.float32), 0.5, 1.5).astype(jnp.bfloat16),
        "w_qkv": bell_draw(key_list[6], (D, 3 * D), D ** -0.5, 0.125, ((0, 4),)),
        "query_gain": jnp.clip(1.0 + 0.1 * jax.random.normal(key_list[7], (HEAD_DIM,), jnp.float32), 0.5, 1.5).astype(jnp.bfloat16),
        "key_gain": jnp.clip(1.0 + 0.1 * jax.random.normal(key_list[8], (HEAD_DIM,), jnp.float32), 0.5, 1.5).astype(jnp.bfloat16),
        "w_out": bell_draw(key_list[9], (D, D), (D // 16) ** -0.5, 0.5, ((0, 4),)),
        "ffn_gain": jnp.clip(1.0 + 0.1 * jax.random.normal(key_list[10], (D,), jnp.float32), 0.5, 1.5).astype(jnp.bfloat16),
        "w_router": bell_draw(key_list[11], (D, EXPERTS), (4 * D) ** -0.5, 0.0625, ((0, 4),)),
        "w_gate_up": bell_draw(key_list[12], (EXPERTS, 2, D, EXPERT_FF), D ** -0.5, 0.125, ((0, 8), (3, 4))),
        "w_down": bell_draw(key_list[13], (EXPERTS, EXPERT_FF, D), 1 ** -0.5, 6.0, ((0, 8), (1, 4))),
    }


EPS = 1e-06
THETA = 50000.0
NEG_BIG = -1e+30

@jax.custom_vjp
def low(v):
    return lax.optimization_barrier(v.astype(jnp.bfloat16)).astype(jnp.float32)

@jax.custom_vjp
def low_back(v):
    return v

def low_keep(v):
    return (low(v), None)

def low_pass(kept, grad):
    return (grad,)

def back_keep(v):
    return (v, None)

def back_low(kept, grad):
    return (low(grad),)
low.defvjp(low_keep, low_pass)
low_back.defvjp(back_keep, back_low)

def rms_normal(values):
    return values * lax.rsqrt(lax.optimization_barrier(jnp.mean(values * values, axis=-1, keepdims=True)) + EPS)

def rotate(values, cosines, sines, factor):
    half_size = values.shape[-1] // 2
    first_half = values[..., :half_size]
    second_half = values[..., half_size:]
    return jnp.concatenate([first_half * cosines - factor * second_half * sines, second_half * cosines + factor * first_half * sines], axis=-1)

def slot_tables(routes, capacity):
    block_count = TOKENS // TOK_DEV
    blocked = routes.reshape(block_count, TOK_DEV * TOPK)

    def block_slots(flat_routes):
        one_hot = (flat_routes[:, None] == jnp.arange(EXPERTS, dtype=jnp.int32)[None, :]).astype(jnp.int32)
        earlier = lax.optimization_barrier(jnp.sum((jnp.cumsum(one_hot, axis=0) - one_hot) * one_hot, axis=-1))
        kept_mask = earlier < capacity[flat_routes]
        slot_index = jnp.where(kept_mask, flat_routes * CAP + earlier, EXPERTS * CAP).astype(jnp.int32)
        pair_token = (jnp.arange(TOK_DEV * TOPK, dtype=jnp.int32) // TOPK).astype(jnp.int32)
        source = jnp.full((EXPERTS * CAP + 1,), TOK_DEV, jnp.int32).at[slot_index].set(pair_token)[:EXPERTS * CAP]
        pair_slot = jnp.where(kept_mask, slot_index, 0).astype(jnp.int32)
        return (source, pair_slot.reshape(TOK_DEV, TOPK), kept_mask.reshape(TOK_DEV, TOPK))
    return jax.vmap(block_slots)(blocked)

def sequence_mix(packed):
    queries, keyed, valued, doc_ids = packed
    highest = lax.Precision.HIGHEST
    scores = low_back(jnp.einsum('qhd,khd->hqk', queries, keyed, precision=highest) * HEAD_DIM ** (-0.5))
    same_doc = doc_ids[:, None] == doc_ids[None, :]
    scores = jnp.where(same_doc[None], scores, NEG_BIG)
    probs = low(jax.nn.softmax(scores, axis=-1))
    return jnp.einsum('hqk,khd->qhd', probs, valued, precision=highest)

def expert_block(block_in, block_weight, source, pair_slot, gate_up_weight, down_weight):
    highest = lax.Precision.HIGHEST
    padded = jnp.concatenate([block_in, jnp.zeros((1, D), block_in.dtype)], axis=0)
    slot_rows = low_back(padded[source]).reshape(EXPERTS, CAP, D)
    pre_gate = low_back(jnp.einsum('ecd,edf->ecf', slot_rows, gate_up_weight[:, 0], precision=highest))
    pre_up = low_back(jnp.einsum('ecd,edf->ecf', slot_rows, gate_up_weight[:, 1], precision=highest))
    activated = low(jax.nn.silu(pre_gate) * pre_up)
    expert_out = low_back(low(jnp.einsum('ecf,efd->ecd', activated, down_weight, precision=highest)))
    pair_out = expert_out.reshape(EXPERTS * CAP, D)[pair_slot]
    return lax.optimization_barrier(jnp.sum(block_weight[:, :, None] * pair_out, axis=1))

def reference(tokens, out_grad, routes, segments, capacity, attn_gain, w_qkv, query_gain, key_gain, w_out, ffn_gain, w_router, w_gate_up, w_down):
    source, pair_slot, kept = slot_tables(routes, capacity)
    kept_float = kept.reshape(TOKENS, TOPK).astype(jnp.float32)
    block_count = TOKENS // TOK_DEV
    seq_length = TOK_DEV * N_SHARD
    half_size = HEAD_DIM // 2
    position = (jnp.arange(TOKENS, dtype=jnp.int32) % seq_length).astype(jnp.float32)
    frequency = THETA ** (-(2.0 * jnp.arange(half_size, dtype=jnp.float32)) / HEAD_DIM)
    angles = position[:, None] * frequency[None, :]
    cosines = jnp.cos(angles)[:, None, :]
    sines = jnp.sin(angles)[:, None, :]
    doc_ids = segments.reshape(N_EXPERT, seq_length)

    def forward(tok_float, gain_one, qkv_weight, gain_query, gain_key, out_weight, gain_two, router_weight, gate_up_weight, down_weight):
        highest = lax.Precision.HIGHEST
        normed = low(rms_normal(tok_float) * gain_one)
        qkv_pre = low_back(jnp.dot(normed, qkv_weight, precision=highest))
        query_pre = qkv_pre[:, :D].reshape(TOKENS, HEADS, HEAD_DIM)
        key_pre = qkv_pre[:, D:2 * D].reshape(TOKENS, HEADS, HEAD_DIM)
        value_pre = qkv_pre[:, 2 * D:].reshape(TOKENS, HEADS, HEAD_DIM)
        queries = low_back(low(rotate(rms_normal(query_pre) * gain_query, cosines, sines, 1.0)))
        keyed = low_back(low(rotate(rms_normal(key_pre) * gain_key, cosines, sines, 1.0)))
        valued = low_back(low(value_pre))
        seq_shape = (N_EXPERT, seq_length, HEADS, HEAD_DIM)
        mixed_heads = lax.map(jax.checkpoint(sequence_mix), (queries.reshape(seq_shape), keyed.reshape(seq_shape), valued.reshape(seq_shape), doc_ids))
        mixed = low_back(low(mixed_heads.reshape(TOKENS, D)))
        hidden = tok_float + low_back(jnp.dot(mixed, out_weight, precision=highest))
        ffn_in = low(rms_normal(hidden) * gain_two)
        router = jax.nn.softmax(low_back(jnp.dot(ffn_in, router_weight, precision=highest)), axis=-1)
        gate_values = jnp.take_along_axis(router, routes, axis=1) * kept_float

        def block_moe(packed):
            return expert_block(packed[0], packed[1], packed[2], packed[3], gate_up_weight, down_weight)
        expert_mix = lax.map(jax.checkpoint(block_moe), (ffn_in.reshape(block_count, TOK_DEV, D), gate_values.reshape(block_count, TOK_DEV, TOPK), source, pair_slot))
        return hidden + expert_mix.reshape(TOKENS, D)
    params = tuple((entry.astype(jnp.float32) for entry in (tokens, attn_gain, w_qkv, query_gain, key_gain, w_out, ffn_gain, w_router, w_gate_up, w_down)))
    result, pullback = jax.vjp(forward, *params)
    grads = pullback(out_grad.astype(jnp.float32))
    return (result.astype(jnp.bfloat16), grads[0], grads[1], grads[2], grads[3], grads[4], grads[5], grads[6], grads[7], grads[8], grads[9])
```

```python
import functools

import jax
import jax.numpy as jnp
from jax import lax
from jax.experimental import pallas as pl
from jax.experimental.pallas import tpu as pltpu
from jax.sharding import PartitionSpec as P

HEADS = 16
EPS = 1e-06
THETA = 50000.0
NEG_BIG = -1e30
F32 = jnp.float32
BF16 = jnp.bfloat16


def dot_f32(left, right, dims):
    return lax.dot_general(left, right, (dims, ((), ())), preferred_element_type=F32)


def rms_scale(values):
    return lax.rsqrt(jnp.mean(values * values, axis=-1, keepdims=True) + EPS)


def norm_back(grad_in, values, scale, gain):
    weighted = grad_in * gain
    return scale * weighted - values * scale**3 * jnp.mean(
        weighted * values, axis=-1, keepdims=True
    )


def ring_order(size):
    if size == 8:
        return [0, 2, 4, 6, 7, 5, 3, 1]
    return list(range(size))


def ring_perms(size):
    order = ring_order(size)
    ahead = [(order[i], order[(i + 1) % size]) for i in range(size)]
    return ahead, [(b, a) for a, b in ahead]


def ring_place(size):
    order = ring_order(size)
    places = [0] * size
    for place, index in enumerate(order):
        places[index] = place
    mine = jnp.array(places, jnp.int32)[lax.axis_index("expert")]
    source = jnp.array(order, jnp.int32)[
        jnp.mod(mine - jnp.arange(size, dtype=jnp.int32), size)
    ]
    return mine, source


def tied(value, *others):
    return lax.optimization_barrier((value, others))[0]


def ring_gather(block, size):
    ahead, back = ring_perms(size)
    half = block.shape[0] // 2
    blocks = [block] * size
    from_behind = from_ahead = block
    for step in range(1, size // 2):
        from_behind = lax.ppermute(from_behind, "expert", ahead)
        from_ahead = lax.ppermute(from_ahead, "expert", back)
        blocks[step] = from_behind
        blocks[size - step] = from_ahead
    top = lax.ppermute(from_behind[:half], "expert", ahead)
    bottom = lax.ppermute(from_ahead[half:], "expert", back)
    blocks[size // 2] = jnp.concatenate([top, bottom], axis=0)
    return blocks


def arrivals(size):
    order = [0]
    for step in range(1, size // 2):
        order += [step, size - step]
    return order + [size // 2]


def ring_scatter(pick, size):
    ahead, back = ring_perms(size)
    first = pick(size // 2)
    half = first.shape[0] // 2
    down = lax.ppermute(first[:half].astype(BF16), "expert", back)
    up = lax.ppermute(first[half:].astype(BF16), "expert", ahead)
    hops = [down]
    for step in range(size // 2 - 1, 0, -1):
        own_down, own_up = pick(step).astype(F32), pick(size - step).astype(F32)
        if step == size // 2 - 1:
            zeros = jnp.zeros_like(down)
            down = jnp.concatenate([down, zeros], axis=0)
            up = jnp.concatenate([zeros, up], axis=0)
        down = lax.ppermute((own_down + down.astype(F32)).astype(BF16), "expert", back)
        up = lax.ppermute((own_up + up.astype(F32)).astype(BF16), "expert", ahead)
        hops.append(down)
    return pick(0).astype(F32) + down.astype(F32) + up.astype(F32), hops


def swap(value, bit):
    size = lax.axis_size("shard")
    return lax.ppermute(value, "shard", [(i, i ^ bit) for i in range(size)])


def shard_gather(block):
    far = swap(block, 2)
    near = swap(block, 1)
    return [block, near, far, swap(far, 1)]


def shard_scatter(blocks):
    near = [swap(blocks[3].astype(BF16), 1), swap(blocks[1].astype(BF16), 1)]
    far = swap((blocks[2].astype(F32) + near[0].astype(F32)).astype(BF16), 2)
    return blocks[0].astype(F32) + near[1].astype(F32) + far.astype(F32)


def tree_sum(value, axis):
    size = lax.axis_size(axis)
    bit = 1
    while bit < size:
        value = value + lax.ppermute(value, axis, [(i, i ^ bit) for i in range(size)])
        bit *= 2
    return value


def turned(values, cosines, sines):
    return values * cosines + pltpu.roll(values, values.shape[-1] // 2, 1) * sines


def attention_kernel(scale, chunk, q_ref, k_ref, v_ref, cos_ref, sin_ref, col_ref, row_ref, gq_ref, gk_ref, out_ref):
    cosines, sines = cos_ref[...], sin_ref[...]
    q_pre, k_pre = q_ref[...], k_ref[...]
    query = turned(q_pre * rms_scale(q_pre) * gq_ref[...], cosines, sines).astype(BF16)
    key = turned(k_pre * rms_scale(k_pre) * gk_ref[...], cosines, sines).astype(BF16)
    value = v_ref[...].astype(BF16)
    docs = row_ref[...]
    for start in range(0, q_pre.shape[0], chunk):
        rows = slice(start, start + chunk)
        scores = dot_f32(query[rows], key, ((1,), (1,))) * scale
        scores = jnp.where(col_ref[rows, :] == docs, scores, NEG_BIG)
        shifted = jnp.exp(scores - jnp.max(scores, axis=-1, keepdims=True))
        probs = shifted * (1.0 / jnp.sum(shifted, axis=-1, keepdims=True))
        out_ref[rows, :] = dot_f32(probs.astype(BF16), value, ((1,), (0,))).astype(BF16)


def attention_back_kernel(
    scale, chunk, q_ref, k_ref, v_ref, do_ref, cos_ref, sin_ref, col_ref, row_ref, gq_ref, gk_ref,
    dq_ref, dk_ref, dv_ref, gains_ref, dq_acc, dk_acc, dv_acc,
):
    cosines, sines = cos_ref[...], sin_ref[...]
    q_pre, k_pre = q_ref[...], k_ref[...]
    q_scale, k_scale = rms_scale(q_pre), rms_scale(k_pre)
    query = turned(q_pre * q_scale * gq_ref[...], cosines, sines).astype(BF16)
    key = turned(k_pre * k_scale * gk_ref[...], cosines, sines).astype(BF16)
    value = v_ref[...].astype(BF16)
    docs = row_ref[...]
    for start in range(0, q_pre.shape[0], chunk):
        rows = slice(start, start + chunk)
        out_back = do_ref[rows, :]
        scores = dot_f32(query[rows], key, ((1,), (1,))) * scale
        scores = jnp.where(col_ref[rows, :] == docs, scores, NEG_BIG)
        shifted = jnp.exp(scores - jnp.max(scores, axis=-1, keepdims=True))
        probs = shifted * (1.0 / jnp.sum(shifted, axis=-1, keepdims=True))
        prob_back = dot_f32(out_back, value, ((1,), (1,)))
        score_back = (
            probs * (prob_back - jnp.sum(probs * prob_back, axis=-1, keepdims=True))
        ).astype(BF16)
        dq_acc[rows, :] = dot_f32(score_back, key, ((1,), (0,)))
        dk_part = dot_f32(score_back, query[rows], ((0,), (0,)))
        dv_part = dot_f32(probs.astype(BF16), out_back, ((0,), (0,)))
        if start == 0:
            dk_acc[...] = dk_part
            dv_acc[...] = dv_part
        else:
            dk_acc[...] += dk_part
            dv_acc[...] += dv_part
    dv_ref[...] = dv_acc[...].astype(BF16)

    @pl.when(pl.program_id(0) == 0)
    def _():
        gains_ref[...] = jnp.zeros_like(gains_ref)

    for place, (acc, pre, pre_scale, gain, out) in enumerate(
        (
            (dq_acc, q_pre, q_scale, gq_ref[...], dq_ref),
            (dk_acc, k_pre, k_scale, gk_ref[...], dk_ref),
        )
    ):
        grad = turned((acc[...] * scale).astype(BF16).astype(F32), cosines, -sines)
        gains_ref[place : place + 1, :] += jnp.sum(grad * pre * pre_scale, axis=0, keepdims=True)
        out[...] = norm_back(grad, pre, pre_scale, gain).astype(BF16)


def attention_specs(length, size, heads):
    def column(part):
        return pl.BlockSpec((length, size), lambda h: (0, part * heads + h))

    def whole(*shape):
        return pl.BlockSpec(shape, lambda h: (0, 0))

    pre = [column(0), column(1), column(2)]
    rest = [
        whole(length, size),
        whole(length, size),
        whole(length, 1),
        whole(1, length),
        whole(1, size),
        whole(1, size),
    ]
    return column(0), pre, rest


def attention(qkv_pre, tables, heads, size):
    length = qkv_pre.shape[0]
    own, pre, rest = attention_specs(length, size, heads)
    return pl.pallas_call(
        functools.partial(attention_kernel, size**-0.5, min(256, length)),
        grid=(heads,),
        in_specs=pre + rest,
        out_specs=own,
        out_shape=jax.ShapeDtypeStruct((length, heads * size), BF16),
        cost_estimate=pl.CostEstimate(
            flops=4 * heads * length * length * size,
            bytes_accessed=qkv_pre.size * 4 + length * heads * size * 2,
            transcendentals=heads * length * length,
        ),
        name="attention",
    )(qkv_pre, qkv_pre, qkv_pre, *tables)


def attention_back(qkv_pre, head_back, tables, heads, size):
    length = qkv_pre.shape[0]
    own, pre, rest = attention_specs(length, size, heads)
    shape = jax.ShapeDtypeStruct((length, heads * size), BF16)
    return pl.pallas_call(
        functools.partial(attention_back_kernel, size**-0.5, min(256, length)),
        grid=(heads,),
        in_specs=pre + [own] + rest,
        out_specs=[own, own, own, pl.BlockSpec((2, size), lambda h: (0, 0))],
        out_shape=[shape, shape, shape, jax.ShapeDtypeStruct((2, size), F32)],
        scratch_shapes=[pltpu.VMEM((length, size), F32)] * 3,
        cost_estimate=pl.CostEstimate(
            flops=10 * heads * length * length * size,
            bytes_accessed=qkv_pre.size * 4 + 4 * length * heads * size * 2,
            transcendentals=heads * length * length,
        ),
        name="attention_back",
    )(qkv_pre, qkv_pre, qkv_pre, head_back, *tables)


GROUP = 4
VMEM_BYTES = 60 * 1024 * 1024


def expert_kernel(count, base_ref, *refs):
    x_refs, dy_refs = refs[:count], refs[count : 2 * count]
    slot_ref, router_ref, wg_ref, wu_ref, wd_ref = refs[2 * count : 2 * count + 5]
    rin_ref, rcot_ref, act_ref, gb_ref, ub_ref, terms_ref, rback_ref = refs[
        2 * count + 5 : 2 * count + 12
    ]
    acc_ref, sum_ref, weight_ref, gg_ref = refs[2 * count + 12 :]
    expert, part = pl.program_id(0), pl.program_id(1)
    tokens = x_refs[0].shape[0]
    slots = rin_ref.shape[1] // count

    def pick_of(block):
        places = lax.broadcasted_iota(jnp.int32, (slots, tokens), 0)
        return places == slot_ref[0, block : block + 1, :]

    def low(mask):
        return jnp.where(mask, 1.0, 0.0).astype(BF16)

    @pl.when(part == 0)
    def _():
        mine = base_ref[0] + expert
        for block in range(count):
            rows = pl.ds(block * slots, slots)
            pick = pick_of(block)
            pick_low = low(pick)
            x_block = x_refs[block][...]
            rin_ref[0, rows, :] = dot_f32(pick_low, x_block, ((1,), (0,))).astype(BF16)
            rcot_ref[0, rows, :] = dot_f32(
                pick_low, dy_refs[block][...], ((1,), (0,))
            ).astype(BF16)
            logits = dot_f32(router_ref[...], x_block, ((1,), (1,)))
            powers = jnp.exp(logits - jnp.max(logits, axis=0, keepdims=True))
            router = powers / jnp.sum(powers, axis=0, keepdims=True)
            which = lax.broadcasted_iota(jnp.int32, router.shape, 0)
            gate = jnp.sum(jnp.where(which == mine, router, 0.0), axis=0, keepdims=True)
            weight_ref[rows, :] = jnp.sum(
                jnp.where(pick, gate, 0.0), axis=1, keepdims=True
            )

    rows_in, rows_cot = rin_ref[0], rcot_ref[0]
    w_gate, w_up, w_back = wg_ref[0, 0], wu_ref[0, 0], wd_ref[0, 0]
    weight = weight_ref[...]
    pre_gate = dot_f32(rows_in, w_gate, ((1,), (0,)))
    pre_up = dot_f32(rows_in, w_up, ((1,), (0,)))
    cot_down = dot_f32(rows_cot, w_back, ((1,), (1,)))
    sigmoid = jax.nn.sigmoid(pre_gate)
    silu = pre_gate * sigmoid
    act = silu * pre_up
    share = act * cot_down
    folded = share[:, :128]
    for lane in range(128, share.shape[1], 128):
        folded = folded + share[:, lane : lane + 128]
    act_back = weight * cot_down
    gate_back = (act_back * pre_up * (sigmoid + silu * (1.0 - sigmoid))).astype(BF16)
    up_back = (act_back * silu).astype(BF16)
    act_ref[0] = (weight * act).astype(BF16)
    gb_ref[0] = gate_back
    ub_ref[0] = up_back
    back = dot_f32(gate_back, w_gate, ((1,), (1,))) + dot_f32(up_back, w_up, ((1,), (1,)))

    @pl.when(part == 0)
    def _():
        gg_ref[...] = folded
        acc_ref[...] = back

    @pl.when(part > 0)
    def _():
        gg_ref[...] += folded
        acc_ref[...] += back

    @pl.when(part == pl.num_programs(1) - 1)
    def _():
        for block in range(count):
            rows = pl.ds(block * slots, slots)
            pick = pick_of(block)
            share = jnp.sum(gg_ref[rows, :], axis=1, keepdims=True)
            rback_ref[0, block : block + 1, :] = jnp.sum(
                jnp.where(pick, share, 0.0), axis=0, keepdims=True
            )
            term = dot_f32(low(pick), acc_ref[rows, :].astype(BF16), ((0,), (0,)))

            @pl.when(expert == 0)
            def _():
                sum_ref[block] = term

            @pl.when(expert > 0)
            def _():
                sum_ref[block] += term

            @pl.when(expert == pl.num_programs(0) - 1)
            def _():
                terms_ref[block] = sum_ref[block].astype(BF16)


def weight_spec(shape):
    return pl.BlockSpec((1, 1) + shape[2:], lambda e, j: (j, e, 0, 0))


def expert_group(base, x_blocks, dy_blocks, slot_of, router_rows, w_gate, w_up, w_down, slots):
    count = len(x_blocks)
    tokens, width = x_blocks[0].shape
    parts, experts, hidden = w_down.shape[:3]
    rows = count * slots

    def still(shape):
        return pl.BlockSpec(
            shape, lambda e, j: (0,) * len(shape), pipeline_mode=pl.Buffered(1)
        )

    def per_expert(*shape):
        return pl.BlockSpec((1,) + shape, lambda e, j: (e, 0, 0))

    part = pl.BlockSpec((1, rows, hidden), lambda e, j: (e, 0, j))
    wide = jax.ShapeDtypeStruct((experts, rows, width), BF16)
    deep = jax.ShapeDtypeStruct((experts, rows, parts * hidden), BF16)
    flops = 10 * rows * width * parts * hidden * experts
    return pl.pallas_call(
        functools.partial(expert_kernel, count),
        grid=(experts, parts),
        in_specs=[pl.BlockSpec(memory_space=pltpu.SMEM)]
        + [still((tokens, width))] * (2 * count)
        + [
            per_expert(count, tokens),
            still(router_rows.shape),
            weight_spec(w_gate.shape),
            weight_spec(w_up.shape),
            weight_spec(w_down.shape),
        ],
        out_specs=[
            per_expert(rows, width),
            per_expert(rows, width),
            part,
            part,
            part,
            pl.BlockSpec(
                (count, tokens, width), lambda e, j: (0, 0, 0), pipeline_mode=pl.Buffered(1)
            ),
            per_expert(count, tokens),
        ],
        out_shape=[
            wide,
            wide,
            deep,
            deep,
            deep,
            jax.ShapeDtypeStruct((count, tokens, width), BF16),
            jax.ShapeDtypeStruct((experts, count, tokens), F32),
        ],
        scratch_shapes=[
            pltpu.VMEM((rows, width), F32),
            pltpu.VMEM((count, tokens, width), F32),
            pltpu.VMEM((rows, 1), F32),
            pltpu.VMEM((rows, 128), F32),
        ],
        compiler_params=pltpu.CompilerParams(vmem_limit_bytes=VMEM_BYTES),
        cost_estimate=pl.CostEstimate(
            flops=flops, bytes_accessed=6 * w_gate.size, transcendentals=rows * parts * hidden
        ),
        name="experts",
    )(base, *x_blocks, *dy_blocks, slot_of, router_rows, w_gate, w_up, w_down)


def output_kernel(count, slot_ref, act_ref, wd_ref, terms_ref, acc_ref, sum_ref):
    expert, part = pl.program_id(0), pl.program_id(1)
    tokens = terms_ref.shape[1]
    slots = act_ref.shape[1] // count
    out = dot_f32(act_ref[0], wd_ref[0, 0], ((1,), (0,)))

    @pl.when(part == 0)
    def _():
        acc_ref[...] = out

    @pl.when(part > 0)
    def _():
        acc_ref[...] += out

    @pl.when(part == pl.num_programs(1) - 1)
    def _():
        for block in range(count):
            places = lax.broadcasted_iota(jnp.int32, (slots, tokens), 0)
            pick = jnp.where(places == slot_ref[0, block : block + 1, :], 1.0, 0.0).astype(BF16)
            rows = acc_ref[pl.ds(block * slots, slots), :].astype(BF16)
            term = dot_f32(pick, rows, ((0,), (0,)))

            @pl.when(expert == 0)
            def _():
                sum_ref[block] = term

            @pl.when(expert > 0)
            def _():
                sum_ref[block] += term

            @pl.when(expert == pl.num_programs(0) - 1)
            def _():
                terms_ref[block] = sum_ref[block].astype(BF16)


def expert_output(slot_of, act, w_down):
    experts, count, tokens = slot_of.shape
    parts, _, hidden, width = w_down.shape
    rows = act.shape[1]
    return pl.pallas_call(
        functools.partial(output_kernel, count),
        grid=(experts, parts),
        in_specs=[
            pl.BlockSpec((1, count, tokens), lambda e, j: (e, 0, 0)),
            pl.BlockSpec((1, rows, hidden), lambda e, j: (e, 0, j)),
            weight_spec(w_down.shape),
        ],
        out_specs=pl.BlockSpec((count, tokens, width), lambda e, j: (0, 0, 0)),
        out_shape=jax.ShapeDtypeStruct((count, tokens, width), BF16),
        scratch_shapes=[
            pltpu.VMEM((rows, width), F32),
            pltpu.VMEM((count, tokens, width), F32),
        ],
        compiler_params=pltpu.CompilerParams(vmem_limit_bytes=VMEM_BYTES),
        cost_estimate=pl.CostEstimate(
            flops=2 * rows * width * parts * hidden * experts,
            bytes_accessed=2 * (w_down.size + act.size + count * tokens * width),
            transcendentals=0,
        ),
        name="expert_output",
    )(slot_of, act, w_down)


def grad_kernel(groups, *refs):
    total = None
    for left, right in zip(refs[:groups], refs[groups : 2 * groups]):
        part = dot_f32(left[0], right[0], ((0,), (0,)))
        total = part if total is None else total + part
    refs[-1][0, 0] = total.astype(BF16)


def expert_grad(lefts, rights, parts):
    experts = lefts[0].shape[0]
    hidden = min(lefts[0].shape[2], rights[0].shape[2]) // parts

    def spec(array, cut):
        width = hidden if cut else array.shape[2]
        return pl.BlockSpec(
            (1, array.shape[1], width), lambda e, j: (e, 0, j if cut else 0)
        )

    cut_left = lefts[0].shape[2] < rights[0].shape[2]
    shape = (
        hidden if cut_left else lefts[0].shape[2],
        rights[0].shape[2] if cut_left else hidden,
    )
    rows = sum(left.shape[1] for left in lefts)
    return pl.pallas_call(
        functools.partial(grad_kernel, len(lefts)),
        grid=(experts, parts),
        in_specs=[spec(left, cut_left) for left in lefts]
        + [spec(right, not cut_left) for right in rights],
        out_specs=pl.BlockSpec((1, 1) + shape, lambda e, j: (j, e, 0, 0)),
        out_shape=jax.ShapeDtypeStruct((parts, experts) + shape, BF16),
        compiler_params=pltpu.CompilerParams(vmem_limit_bytes=VMEM_BYTES),
        cost_estimate=pl.CostEstimate(
            flops=2 * rows * shape[0] * shape[1] * parts * experts,
            bytes_accessed=2 * experts * (parts * shape[0] * shape[1] + 3 * rows * shape[0]),
            transcendentals=0,
        ),
        name="expert_grad",
    )(*lefts, *rights)


def on_device(
    tokens,
    out_grad,
    routes,
    segments,
    capacity,
    attn_gain,
    w_qkv,
    query_gain,
    key_gain,
    w_out,
    ffn_gain,
    w_router,
    w_gate_up,
    w_down,
):
    n_expert = lax.axis_size("expert")
    n_shard = lax.axis_size("shard")
    rows, width = tokens.shape
    size = width // HEADS
    heads = HEADS // n_shard
    local_width = heads * size
    length = segments.shape[0]
    expert_count = capacity.shape[0]
    local_experts = w_down.shape[0]
    slots = rows * routes.shape[1] // expert_count
    shard_index = lax.axis_index("shard")
    expert_index = lax.axis_index("expert")
    place, source = ring_place(n_expert)
    part_rows = w_qkv.shape[0]
    slice_rows = part_rows // n_expert
    relative = jnp.bitwise_xor(shard_index, jnp.arange(n_shard, dtype=jnp.int32))

    packed = jnp.concatenate(
        [attn_gain, ffn_gain, query_gain, key_gain, w_router.reshape(-1)]
    )
    packed = lax.all_to_all(
        jnp.broadcast_to(packed[None], (n_shard, packed.shape[0])), "shard", 0, 0, tiled=True
    )
    cuts = [part_rows, 2 * part_rows, 2 * part_rows + size // n_shard]
    cuts.append(cuts[-1] + size // n_shard)
    gain_one = packed[:, : cuts[0]].reshape(1, width).astype(F32)
    gain_two = packed[:, cuts[0] : cuts[1]].reshape(1, width).astype(F32)
    gain_query = packed[:, cuts[1] : cuts[2]].reshape(1, size).astype(F32)
    gain_key = packed[:, cuts[2] : cuts[3]].reshape(1, size).astype(F32)
    full_router = packed[:, cuts[3] :].reshape(width, expert_count)
    router_rows = full_router.T

    own_slice = lax.dynamic_slice_in_dim(w_qkv, expert_index * slice_rows, slice_rows)
    own_slice = own_slice.reshape(slice_rows, 3, n_shard, local_width).transpose(2, 0, 1, 3)
    own_slice = lax.all_to_all(
        own_slice.reshape(n_shard, slice_rows, 3 * local_width), "shard", 0, 0, tiled=True
    )
    w_blocks = ring_gather(
        own_slice.reshape(n_shard * slice_rows, 3 * local_width), n_expert
    )
    w_local = jnp.zeros((n_shard, n_expert, slice_rows, 3 * local_width), BF16)
    for r in arrivals(n_expert):
        w_local = lax.dynamic_update_slice(
            w_local,
            w_blocks[r].reshape(n_shard, 1, slice_rows, 3 * local_width),
            (0, source[r], 0, 0),
        )
    w_local = w_local.reshape(width, 3 * local_width)

    token_parts = shard_gather(tokens)
    token_blocks = jnp.concatenate(token_parts, axis=0)

    dy_blocks = ring_gather(tied(out_grad, w_blocks[n_expert // 2]), n_expert)
    routes_all = lax.all_to_all(
        jnp.broadcast_to(routes[None], (n_expert,) + routes.shape), "expert", 0, 0, tiled=True
    )[source]

    gate_own, up_own = w_gate_up[:, 0], w_gate_up[:, 1]
    gate_full = jnp.stack(shard_gather(tied(gate_own, token_parts[2])))
    up_full = jnp.stack(shard_gather(tied(up_own, token_parts[2])))

    my_experts = expert_index * local_experts + jnp.arange(local_experts, dtype=jnp.int32)
    named = jnp.any(
        routes_all[None, :, :, :] == my_experts[:, None, None, None], axis=3
    )
    order = jnp.arange(rows, dtype=jnp.int32)
    before = (order[:, None] < order[None, :]).astype(BF16)
    earlier = jnp.einsum(
        "ebu,ut->ebt", named.astype(BF16), before, preferred_element_type=F32
    ).astype(jnp.int32)
    my_limits = lax.dynamic_slice_in_dim(capacity, expert_index * local_experts, local_experts)
    slot_of = jnp.where(named & (earlier < my_limits[:, None, None]), earlier, -1)

    position = (
        relative[:, None] * rows + jnp.arange(rows, dtype=jnp.int32)[None, :]
    ).reshape(-1).astype(F32)
    half_size = size // 2
    frequency = THETA ** (-(2.0 * jnp.arange(half_size, dtype=F32)) / size)
    angles = position[:, None] * frequency[None, :]
    cosines, sines = jnp.cos(angles), jnp.sin(angles)
    docs = segments.reshape(n_shard, rows)[relative].reshape(-1)
    tables = (
        jnp.concatenate([cosines, cosines], axis=1),
        jnp.concatenate([-sines, sines], axis=1),
        docs[:, None],
        docs[None, :],
        gain_query,
        gain_key,
    )

    token_float = token_blocks.astype(F32)
    scale_one = rms_scale(token_float)
    normed = (token_float * scale_one * gain_one).astype(BF16)
    qkv_pre = jnp.dot(normed, w_local, preferred_element_type=F32)
    mixed = attention(qkv_pre, tables, heads, size)
    attended = jnp.dot(mixed, w_out, preferred_element_type=F32).astype(BF16)
    own_tokens = tokens.astype(F32)
    hidden = own_tokens + shard_scatter(list(attended.reshape(n_shard, rows, width)))
    scale_two = rms_scale(hidden)
    ffn_low = (hidden * scale_two * gain_two).astype(BF16)
    router = jax.nn.softmax(
        jnp.dot(ffn_low, full_router, preferred_element_type=F32), axis=-1
    )
    down_full = jnp.stack(shard_gather(tied(w_down, ffn_low)))

    ffn_blocks = ring_gather(ffn_low, n_expert)
    arrival = arrivals(n_expert)
    groups = [arrival[i : i + GROUP] for i in range(0, n_expert, GROUP)]
    base = (expert_index * local_experts).reshape(1).astype(jnp.int32)
    results, slot_groups = [], []
    for group in groups:
        slot_groups.append(jnp.stack([slot_of[:, r] for r in group], axis=1))
        results.append(
            expert_group(
                base,
                [ffn_blocks[r] for r in group],
                [dy_blocks[r] for r in group],
                slot_groups[-1],
                router_rows,
                gate_full,
                up_full,
                down_full,
                slots,
            )
        )
    rows_in, rows_cot, act, gate_back, up_back, terms, router_terms = map(list, zip(*results))
    where_is = {r: (g, i) for g, group in enumerate(groups) for i, r in enumerate(group)}

    def picker(arrays):
        return lambda r: arrays[where_is[r][0]][where_is[r][1]]

    ffn_back, hops = ring_scatter(picker(terms), n_expert)
    to_block = jnp.zeros((n_expert,), jnp.int32).at[source].set(
        jnp.arange(n_expert, dtype=jnp.int32)
    )
    back_to = jnp.stack(
        [router_terms[where_is[r][0]][:, where_is[r][1]] for r in range(n_expert)]
    )
    router_back = lax.all_to_all(
        back_to[to_block], "expert", split_axis=0, concat_axis=0, tiled=True
    ).reshape(expert_count, rows).T

    gate_parts = expert_grad(rows_in, gate_back, n_shard)
    gate_grads = shard_scatter(list(gate_parts))
    up_parts = expert_grad(tied(rows_in, hops[0]), up_back, n_shard)
    up_grads = shard_scatter(list(up_parts))
    down_parts = expert_grad(tied(act, hops[1]), rows_cot, n_shard)
    out_terms = [
        expert_output(slots_g, tied(act_g, hops[2]), down_full)
        for slots_g, act_g in zip(slot_groups, act)
    ]
    out_terms[-1] = tied(out_terms[-1], ffn_back)
    out_sum, _ = ring_scatter(picker(out_terms), n_expert)
    layer_out = (hidden + out_sum).astype(BF16)

    logit_back = (
        router * (router_back - jnp.sum(router * router_back, axis=-1, keepdims=True))
    ).astype(BF16)
    router_grad = dot_f32(ffn_low, logit_back, ((0,), (0,)))
    ffn_back = ffn_back + dot_f32(logit_back, full_router, ((1,), (1,)))
    gain_two_part = jnp.sum(ffn_back * hidden * scale_two, axis=0)
    hidden_back = out_grad.astype(F32) + norm_back(ffn_back, hidden, scale_two, gain_two)

    mix_back = jnp.concatenate(shard_gather(hidden_back.astype(BF16)), axis=0)
    down_grad = shard_scatter(list(tied(down_parts, mix_back)))
    head_back = dot_f32(mix_back, w_out, ((1,), (1,))).astype(BF16)
    out_part = dot_f32(mixed, mix_back, ((0,), (0,))).astype(BF16)
    query_back, key_back, value_back, head_gains = attention_back(
        qkv_pre, head_back, tables, heads, size
    )
    qkv_back = jnp.concatenate([query_back, key_back, value_back], axis=1)
    qkv_part = dot_f32(normed, qkv_back, ((0,), (0,))).astype(BF16)
    normed_back = dot_f32(tied(qkv_back, qkv_part), w_local, ((1,), (1,)))
    gain_one_part = jnp.sum(normed_back * token_float * scale_one, axis=0)
    own_back = shard_scatter(list(normed_back.astype(BF16).reshape(n_shard, rows, width)))
    tokens_grad = hidden_back + norm_back(own_back, own_tokens, scale_one[:rows], gain_one)

    def placed_blocks(blocks):
        total = jnp.zeros((n_expert * blocks[0].shape[0], blocks[0].shape[1]), F32)
        for r in arrivals(n_expert):
            total = lax.dynamic_update_slice(
                total, blocks[r].astype(F32), (source[r] * blocks[r].shape[0], 0)
            )
        return total

    out_terms_w = out_part.reshape(n_expert, slice_rows, width)
    out_mine, _ = ring_scatter(
        lambda r: lax.dynamic_index_in_dim(out_terms_w, source[r], 0, keepdims=False), n_expert
    )
    out_total = placed_blocks(ring_gather(out_mine.astype(BF16), n_expert))
    qkv_terms = qkv_part.reshape(n_shard, n_expert, slice_rows, 3 * local_width)
    qkv_mine, _ = ring_scatter(
        lambda r: lax.dynamic_index_in_dim(qkv_terms, source[r], 1, keepdims=False).reshape(
            n_shard * slice_rows, 3 * local_width
        ),
        n_expert,
    )
    qkv_mine = lax.all_to_all(
        qkv_mine.astype(BF16), "shard", split_axis=0, concat_axis=0, tiled=True
    )
    qkv_mine = (
        qkv_mine.reshape(n_shard, slice_rows, 3, local_width)
        .transpose(1, 2, 0, 3)
        .reshape(slice_rows, 3 * width)
    )
    qkv_total = placed_blocks(ring_gather(qkv_mine, n_expert))

    small = jnp.concatenate(
        [
            gain_one_part.reshape(n_shard, -1),
            gain_two_part.reshape(n_shard, -1),
            head_gains[0].reshape(n_shard, -1),
            head_gains[1].reshape(n_shard, -1),
            router_grad.reshape(n_shard, -1),
        ],
        axis=1,
    )
    small = lax.all_to_all(small, "shard", split_axis=0, concat_axis=0, tiled=True)
    small = tree_sum(jnp.sum(small, axis=0).reshape(1, -1), "expert")[0]
    gate_up_grad = jnp.stack([gate_grads, up_grads], axis=1)
    return (
        layer_out,
        tokens_grad,
        small[: cuts[0]],
        qkv_total,
        small[cuts[1] : cuts[2]],
        small[cuts[2] : cuts[3]],
        out_total,
        small[cuts[0] : cuts[1]],
        small[cuts[3] :].reshape(part_rows, expert_count),
        gate_up_grad,
        down_grad,
    )


def solution(mesh):
    placed = (
        P(("expert", "shard"), None),
        P(("expert", "shard"), None),
        P(("expert", "shard"), None),
        P("expert"),
        P(),
        P("shard"),
        P("shard", None),
        P("shard"),
        P("shard"),
        P("shard", None),
        P("shard"),
        P("shard", None),
        P("expert", None, None, "shard"),
        P("expert", "shard", None),
    )
    return jax.shard_map(
        on_device,
        mesh=mesh,
        in_specs=placed,
        out_specs=(
            P(("expert", "shard"), None),
            P(("expert", "shard"), None),
            P("shard"),
            P("shard", None),
            P("shard"),
            P("shard"),
            P("shard", None),
            P("shard"),
            P("shard", None),
            P("expert", None, None, "shard"),
            P("expert", "shard", None),
        ),
        check_vma=False,
    )
```

```python
import functools

import jax
import jax.numpy as jnp
from jax import lax
from jax.experimental import pallas as pl
from jax.experimental.pallas import tpu as pltpu
from jax.sharding import PartitionSpec as P

HEADS = 16
EPS = 1e-06
THETA = 50000.0
NEG_BIG = -1e30
F32 = jnp.float32
BF16 = jnp.bfloat16


def dot_f32(left, right, dims):
    return lax.dot_general(left, right, (dims, ((), ())), preferred_element_type=F32)


def rms_scale(values):
    return lax.rsqrt(jnp.mean(values * values, axis=-1, keepdims=True) + EPS)


def norm_back(grad_in, values, scale, gain):
    weighted = grad_in * gain
    return scale * weighted - values * scale**3 * jnp.mean(
        weighted * values, axis=-1, keepdims=True
    )


def ring_order(size):
    if size == 8:
        return [0, 2, 4, 6, 7, 5, 3, 1]
    return list(range(size))


def ring_perms(size):
    order = ring_order(size)
    ahead = [(order[i], order[(i + 1) % size]) for i in range(size)]
    return ahead, [(b, a) for a, b in ahead]


def ring_place(size):
    order = ring_order(size)
    places = [0] * size
    for place, index in enumerate(order):
        places[index] = place
    mine = jnp.array(places, jnp.int32)[lax.axis_index("expert")]
    source = jnp.array(order, jnp.int32)[
        jnp.mod(mine - jnp.arange(size, dtype=jnp.int32), size)
    ]
    behind = jnp.mod(mine - jnp.array(places, jnp.int32), size)
    return source, behind


def tied(value, *others):
    return lax.optimization_barrier((value, others))[0]


def ring_gather(block, size):
    ahead, back = ring_perms(size)
    first = (lax.ppermute(block, "expert", ahead), lax.ppermute(block, "expert", back))
    return ring_rest(block, first, size, {})


def ring_rest(block, first, size, gates):
    ahead, back = ring_perms(size)
    half = block.shape[0] // 2
    blocks = [block] * size
    from_behind, from_ahead = first
    blocks[1], blocks[size - 1] = first
    for step in range(2, size // 2):
        if step in gates:
            from_behind, from_ahead = tied((from_behind, from_ahead), gates[step])
        from_behind = lax.ppermute(from_behind, "expert", ahead)
        from_ahead = lax.ppermute(from_ahead, "expert", back)
        blocks[step] = from_behind
        blocks[size - step] = from_ahead
    top = lax.ppermute(from_behind[:half], "expert", ahead)
    bottom = lax.ppermute(from_ahead[half:], "expert", back)
    blocks[size // 2] = jnp.concatenate([top, bottom], axis=0)
    return blocks


def arrivals(size):
    order = [0]
    for step in range(1, size // 2):
        order += [step, size - step]
    return order + [size // 2]


def ring_scatter(pick, size):
    ahead, back = ring_perms(size)
    first = pick(size // 2)
    half = first.shape[0] // 2
    down = lax.ppermute(first[:half].astype(BF16), "expert", back)
    up = lax.ppermute(first[half:].astype(BF16), "expert", ahead)
    hops = [down]
    for step in range(size // 2 - 1, 0, -1):
        own_down, own_up = pick(step).astype(F32), pick(size - step).astype(F32)
        if step == size // 2 - 1:
            zeros = jnp.zeros_like(down)
            down = jnp.concatenate([down, zeros], axis=0)
            up = jnp.concatenate([zeros, up], axis=0)
        down = lax.ppermute((own_down + down.astype(F32)).astype(BF16), "expert", back)
        up = lax.ppermute((own_up + up.astype(F32)).astype(BF16), "expert", ahead)
        hops.append(down)
    return pick(0).astype(F32) + down.astype(F32) + up.astype(F32), hops


def swap(value, bit):
    size = lax.axis_size("shard")
    return lax.ppermute(value, "shard", [(i, i ^ bit) for i in range(size)])


def shard_gather(block):
    far = swap(block, 2)
    near = swap(block, 1)
    return [block, near, far, swap(far, 1)]


def shard_scatter(blocks):
    near = [swap(blocks[3].astype(BF16), 1), swap(blocks[1].astype(BF16), 1)]
    far = swap((blocks[2].astype(F32) + near[0].astype(F32)).astype(BF16), 2)
    return blocks[0].astype(F32) + near[1].astype(F32) + far.astype(F32)


def shard_scatter_late(blocks, gate):
    near = [swap(blocks[3].astype(BF16), 1), swap(blocks[1].astype(BF16), 1)]
    sent = (blocks[2].astype(F32) + near[0].astype(F32)).astype(BF16)
    sent, own = tied((sent, near[1]), gate)
    far = swap(sent, 2)
    return blocks[0].astype(F32) + own.astype(F32) + far.astype(F32), far


def tree_sum(value, axis):
    size = lax.axis_size(axis)
    bit = 1
    while bit < size:
        value = value + lax.ppermute(value, axis, [(i, i ^ bit) for i in range(size)])
        bit *= 2
    return value


def turned(values, cosines, sines):
    return values * cosines + pltpu.roll(values, values.shape[-1] // 2, 1) * sines


def attention_kernel(scale, chunk, q_ref, k_ref, v_ref, cos_ref, sin_ref, col_ref, row_ref, gq_ref, gk_ref, out_ref):
    cosines, sines = cos_ref[...], sin_ref[...]
    q_pre, k_pre = q_ref[...], k_ref[...]
    query = turned(q_pre * rms_scale(q_pre) * gq_ref[...], cosines, sines).astype(BF16)
    key = turned(k_pre * rms_scale(k_pre) * gk_ref[...], cosines, sines).astype(BF16)
    value = v_ref[...].astype(BF16)
    docs = row_ref[...]
    for start in range(0, q_pre.shape[0], chunk):
        rows = slice(start, start + chunk)
        scores = dot_f32(query[rows], key, ((1,), (1,))) * scale
        scores = jnp.where(col_ref[rows, :] == docs, scores, NEG_BIG)
        shifted = jnp.exp(scores - jnp.max(scores, axis=-1, keepdims=True))
        probs = shifted * (1.0 / jnp.sum(shifted, axis=-1, keepdims=True))
        out_ref[rows, :] = dot_f32(probs.astype(BF16), value, ((1,), (0,))).astype(BF16)


def attention_back_kernel(
    scale, chunk, q_ref, k_ref, v_ref, do_ref, cos_ref, sin_ref, col_ref, row_ref, gq_ref, gk_ref,
    dq_ref, dk_ref, dv_ref, gains_ref, dq_acc, dk_acc, dv_acc,
):
    cosines, sines = cos_ref[...], sin_ref[...]
    q_pre, k_pre = q_ref[...], k_ref[...]
    q_scale, k_scale = rms_scale(q_pre), rms_scale(k_pre)
    query = turned(q_pre * q_scale * gq_ref[...], cosines, sines).astype(BF16)
    key = turned(k_pre * k_scale * gk_ref[...], cosines, sines).astype(BF16)
    value = v_ref[...].astype(BF16)
    docs = row_ref[...]
    for start in range(0, q_pre.shape[0], chunk):
        rows = slice(start, start + chunk)
        out_back = do_ref[rows, :]
        scores = dot_f32(query[rows], key, ((1,), (1,))) * scale
        scores = jnp.where(col_ref[rows, :] == docs, scores, NEG_BIG)
        shifted = jnp.exp(scores - jnp.max(scores, axis=-1, keepdims=True))
        probs = shifted * (1.0 / jnp.sum(shifted, axis=-1, keepdims=True))
        prob_back = dot_f32(out_back, value, ((1,), (1,)))
        score_back = (
            probs * (prob_back - jnp.sum(probs * prob_back, axis=-1, keepdims=True))
        ).astype(BF16)
        dq_acc[rows, :] = dot_f32(score_back, key, ((1,), (0,)))
        dk_part = dot_f32(score_back, query[rows], ((0,), (0,)))
        dv_part = dot_f32(probs.astype(BF16), out_back, ((0,), (0,)))
        if start == 0:
            dk_acc[...] = dk_part
            dv_acc[...] = dv_part
        else:
            dk_acc[...] += dk_part
            dv_acc[...] += dv_part
    dv_ref[...] = dv_acc[...].astype(BF16)

    @pl.when(pl.program_id(0) == 0)
    def _():
        gains_ref[...] = jnp.zeros_like(gains_ref)

    for place, (acc, pre, pre_scale, gain, out) in enumerate(
        (
            (dq_acc, q_pre, q_scale, gq_ref[...], dq_ref),
            (dk_acc, k_pre, k_scale, gk_ref[...], dk_ref),
        )
    ):
        grad = turned((acc[...] * scale).astype(BF16).astype(F32), cosines, -sines)
        gains_ref[place : place + 1, :] += jnp.sum(grad * pre * pre_scale, axis=0, keepdims=True)
        out[...] = norm_back(grad, pre, pre_scale, gain).astype(BF16)


def attention_specs(length, size, heads):
    def column(part):
        return pl.BlockSpec((length, size), lambda h: (0, part * heads + h))

    def whole(*shape):
        return pl.BlockSpec(shape, lambda h: (0, 0))

    pre = [column(0), column(1), column(2)]
    rest = [
        whole(length, size),
        whole(length, size),
        whole(length, 1),
        whole(1, length),
        whole(1, size),
        whole(1, size),
    ]
    return column(0), pre, rest


def attention(qkv_pre, tables, heads, size):
    length = qkv_pre.shape[0]
    own, pre, rest = attention_specs(length, size, heads)
    return pl.pallas_call(
        functools.partial(attention_kernel, size**-0.5, min(256, length)),
        grid=(heads,),
        in_specs=pre + rest,
        out_specs=own,
        out_shape=jax.ShapeDtypeStruct((length, heads * size), BF16),
        cost_estimate=pl.CostEstimate(
            flops=4 * heads * length * length * size,
            bytes_accessed=qkv_pre.size * 4 + length * heads * size * 2,
            transcendentals=heads * length * length,
        ),
        name="attention",
    )(qkv_pre, qkv_pre, qkv_pre, *tables)


def attention_back(qkv_pre, head_back, tables, heads, size):
    length = qkv_pre.shape[0]
    own, pre, rest = attention_specs(length, size, heads)
    shape = jax.ShapeDtypeStruct((length, heads * size), BF16)
    return pl.pallas_call(
        functools.partial(attention_back_kernel, size**-0.5, min(256, length)),
        grid=(heads,),
        in_specs=pre + [own] + rest,
        out_specs=[own, own, own, pl.BlockSpec((2, size), lambda h: (0, 0))],
        out_shape=[shape, shape, shape, jax.ShapeDtypeStruct((2, size), F32)],
        scratch_shapes=[pltpu.VMEM((length, size), F32)] * 3,
        cost_estimate=pl.CostEstimate(
            flops=10 * heads * length * length * size,
            bytes_accessed=qkv_pre.size * 4 + 4 * length * heads * size * 2,
            transcendentals=heads * length * length,
        ),
        name="attention_back",
    )(qkv_pre, qkv_pre, qkv_pre, head_back, *tables)


GROUP = 4


def block_groups(size):
    if size == 8:
        return [[0, 1, 7], [4, 3, 5], [2, 6]]
    order = arrivals(size)
    return [order[i : i + GROUP] for i in range(0, size, GROUP)]


VMEM_BYTES = 60 * 1024 * 1024


def expert_kernel(count, base_ref, *refs):
    x_refs, dy_refs = refs[:count], refs[count : 2 * count]
    slot_ref, router_ref, wg_ref, wu_ref, wd_ref = refs[2 * count : 2 * count + 5]
    rin_ref, rcot_ref, act_ref, gb_ref, ub_ref, terms_ref, rback_ref = refs[
        2 * count + 5 : 2 * count + 12
    ]
    acc_ref, sum_ref, weight_ref, gg_ref = refs[2 * count + 12 :]
    expert, part = pl.program_id(0), pl.program_id(1)
    tokens = x_refs[0].shape[0]
    slots = rin_ref.shape[1] // count

    def pick_of(block):
        places = lax.broadcasted_iota(jnp.int32, (slots, tokens), 0)
        return places == slot_ref[0, block : block + 1, :]

    def low(mask):
        return jnp.where(mask, 1.0, 0.0).astype(BF16)

    @pl.when(part == 0)
    def _():
        mine = base_ref[0] + expert
        for block in range(count):
            rows = pl.ds(block * slots, slots)
            pick = pick_of(block)
            pick_low = low(pick)
            x_block = x_refs[block][...]
            rin_ref[0, rows, :] = dot_f32(pick_low, x_block, ((1,), (0,))).astype(BF16)
            rcot_ref[0, rows, :] = dot_f32(
                pick_low, dy_refs[block][...], ((1,), (0,))
            ).astype(BF16)
            logits = dot_f32(router_ref[...], x_block, ((1,), (1,)))
            powers = jnp.exp(logits - jnp.max(logits, axis=0, keepdims=True))
            router = powers / jnp.sum(powers, axis=0, keepdims=True)
            which = lax.broadcasted_iota(jnp.int32, router.shape, 0)
            gate = jnp.sum(jnp.where(which == mine, router, 0.0), axis=0, keepdims=True)
            weight_ref[rows, :] = jnp.sum(
                jnp.where(pick, gate, 0.0), axis=1, keepdims=True
            )

    rows_in, rows_cot = rin_ref[0], rcot_ref[0]
    w_gate, w_up, w_back = wg_ref[0, 0], wu_ref[0, 0], wd_ref[0, 0]
    weight = weight_ref[...]
    pre_gate = dot_f32(rows_in, w_gate, ((1,), (0,)))
    pre_up = dot_f32(rows_in, w_up, ((1,), (0,)))
    cot_down = dot_f32(rows_cot, w_back, ((1,), (1,)))
    sigmoid = jax.nn.sigmoid(pre_gate)
    silu = pre_gate * sigmoid
    act = silu * pre_up
    share = act * cot_down
    folded = share[:, :128]
    for lane in range(128, share.shape[1], 128):
        folded = folded + share[:, lane : lane + 128]
    act_back = weight * cot_down
    gate_back = (act_back * pre_up * (sigmoid + silu * (1.0 - sigmoid))).astype(BF16)
    up_back = (act_back * silu).astype(BF16)
    act_ref[0] = (weight * act).astype(BF16)
    gb_ref[0] = gate_back
    ub_ref[0] = up_back
    back = dot_f32(gate_back, w_gate, ((1,), (1,))) + dot_f32(up_back, w_up, ((1,), (1,)))

    @pl.when(part == 0)
    def _():
        gg_ref[...] = folded
        acc_ref[...] = back

    @pl.when(part > 0)
    def _():
        gg_ref[...] += folded
        acc_ref[...] += back

    @pl.when(part == pl.num_programs(1) - 1)
    def _():
        for block in range(count):
            rows = pl.ds(block * slots, slots)
            pick = pick_of(block)
            share = jnp.sum(gg_ref[rows, :], axis=1, keepdims=True)
            rback_ref[0, block : block + 1, :] = jnp.sum(
                jnp.where(pick, share, 0.0), axis=0, keepdims=True
            )
            term = dot_f32(low(pick), acc_ref[rows, :].astype(BF16), ((0,), (0,)))

            @pl.when(expert == 0)
            def _():
                sum_ref[block] = term

            @pl.when(expert > 0)
            def _():
                sum_ref[block] += term

            @pl.when(expert == pl.num_programs(0) - 1)
            def _():
                terms_ref[block] = sum_ref[block].astype(BF16)


def weight_spec(shape):
    return pl.BlockSpec((1, 1) + shape[2:], lambda e, j: (j, e, 0, 0))


def expert_group(base, x_blocks, dy_blocks, slot_of, router_rows, w_gate, w_up, w_down, slots):
    count = len(x_blocks)
    tokens, width = x_blocks[0].shape
    parts, experts, hidden = w_down.shape[:3]
    rows = count * slots

    def still(shape):
        return pl.BlockSpec(
            shape, lambda e, j: (0,) * len(shape), pipeline_mode=pl.Buffered(1)
        )

    def per_expert(*shape):
        return pl.BlockSpec((1,) + shape, lambda e, j: (e, 0, 0))

    part = pl.BlockSpec((1, rows, hidden), lambda e, j: (e, 0, j))
    wide = jax.ShapeDtypeStruct((experts, rows, width), BF16)
    deep = jax.ShapeDtypeStruct((experts, rows, parts * hidden), BF16)
    flops = 10 * rows * width * parts * hidden * experts
    return pl.pallas_call(
        functools.partial(expert_kernel, count),
        grid=(experts, parts),
        in_specs=[pl.BlockSpec(memory_space=pltpu.SMEM)]
        + [still((tokens, width))] * (2 * count)
        + [
            per_expert(count, tokens),
            still(router_rows.shape),
            weight_spec(w_gate.shape),
            weight_spec(w_up.shape),
            weight_spec(w_down.shape),
        ],
        out_specs=[
            per_expert(rows, width),
            per_expert(rows, width),
            part,
            part,
            part,
            pl.BlockSpec(
                (count, tokens, width), lambda e, j: (0, 0, 0), pipeline_mode=pl.Buffered(1)
            ),
            per_expert(count, tokens),
        ],
        out_shape=[
            wide,
            wide,
            deep,
            deep,
            deep,
            jax.ShapeDtypeStruct((count, tokens, width), BF16),
            jax.ShapeDtypeStruct((experts, count, tokens), F32),
        ],
        scratch_shapes=[
            pltpu.VMEM((rows, width), F32),
            pltpu.VMEM((count, tokens, width), F32),
            pltpu.VMEM((rows, 1), F32),
            pltpu.VMEM((rows, 128), F32),
        ],
        compiler_params=pltpu.CompilerParams(vmem_limit_bytes=VMEM_BYTES),
        cost_estimate=pl.CostEstimate(
            flops=flops, bytes_accessed=6 * w_gate.size, transcendentals=rows * parts * hidden
        ),
        name="experts",
    )(base, *x_blocks, *dy_blocks, slot_of, router_rows, w_gate, w_up, w_down)


def output_kernel(count, slot_ref, act_ref, wd_ref, terms_ref, acc_ref, sum_ref):
    expert, part = pl.program_id(0), pl.program_id(1)
    tokens = terms_ref.shape[1]
    slots = act_ref.shape[1] // count
    out = dot_f32(act_ref[0], wd_ref[0, 0], ((1,), (0,)))

    @pl.when(part == 0)
    def _():
        acc_ref[...] = out

    @pl.when(part > 0)
    def _():
        acc_ref[...] += out

    @pl.when(part == pl.num_programs(1) - 1)
    def _():
        for block in range(count):
            places = lax.broadcasted_iota(jnp.int32, (slots, tokens), 0)
            pick = jnp.where(places == slot_ref[0, block : block + 1, :], 1.0, 0.0).astype(BF16)
            rows = acc_ref[pl.ds(block * slots, slots), :].astype(BF16)
            term = dot_f32(pick, rows, ((0,), (0,)))

            @pl.when(expert == 0)
            def _():
                sum_ref[block] = term

            @pl.when(expert > 0)
            def _():
                sum_ref[block] += term

            @pl.when(expert == pl.num_programs(0) - 1)
            def _():
                terms_ref[block] = sum_ref[block].astype(BF16)


def expert_output(slot_of, act, w_down):
    experts, count, tokens = slot_of.shape
    parts, _, hidden, width = w_down.shape
    rows = act.shape[1]
    return pl.pallas_call(
        functools.partial(output_kernel, count),
        grid=(experts, parts),
        in_specs=[
            pl.BlockSpec((1, count, tokens), lambda e, j: (e, 0, 0)),
            pl.BlockSpec((1, rows, hidden), lambda e, j: (e, 0, j)),
            weight_spec(w_down.shape),
        ],
        out_specs=pl.BlockSpec((count, tokens, width), lambda e, j: (0, 0, 0)),
        out_shape=jax.ShapeDtypeStruct((count, tokens, width), BF16),
        scratch_shapes=[
            pltpu.VMEM((rows, width), F32),
            pltpu.VMEM((count, tokens, width), F32),
        ],
        compiler_params=pltpu.CompilerParams(vmem_limit_bytes=VMEM_BYTES),
        cost_estimate=pl.CostEstimate(
            flops=2 * rows * width * parts * hidden * experts,
            bytes_accessed=2 * (w_down.size + act.size + count * tokens * width),
            transcendentals=0,
        ),
        name="expert_output",
    )(slot_of, act, w_down)


def grad_kernel(groups, *refs):
    total = None
    for left, right in zip(refs[:groups], refs[groups : 2 * groups]):
        part = dot_f32(left[0], right[0], ((0,), (0,)))
        total = part if total is None else total + part
    refs[-1][0, 0] = total.astype(BF16)


def expert_grad(lefts, rights, parts):
    experts = lefts[0].shape[0]
    hidden = min(lefts[0].shape[2], rights[0].shape[2]) // parts

    def spec(array, cut):
        width = hidden if cut else array.shape[2]
        return pl.BlockSpec(
            (1, array.shape[1], width), lambda e, j: (e, 0, j if cut else 0)
        )

    cut_left = lefts[0].shape[2] < rights[0].shape[2]
    shape = (
        hidden if cut_left else lefts[0].shape[2],
        rights[0].shape[2] if cut_left else hidden,
    )
    rows = sum(left.shape[1] for left in lefts)
    return pl.pallas_call(
        functools.partial(grad_kernel, len(lefts)),
        grid=(experts, parts),
        in_specs=[spec(left, cut_left) for left in lefts]
        + [spec(right, not cut_left) for right in rights],
        out_specs=pl.BlockSpec((1, 1) + shape, lambda e, j: (j, e, 0, 0)),
        out_shape=jax.ShapeDtypeStruct((parts, experts) + shape, BF16),
        compiler_params=pltpu.CompilerParams(vmem_limit_bytes=VMEM_BYTES),
        cost_estimate=pl.CostEstimate(
            flops=2 * rows * shape[0] * shape[1] * parts * experts,
            bytes_accessed=2 * experts * (parts * shape[0] * shape[1] + 3 * rows * shape[0]),
            transcendentals=0,
        ),
        name="expert_grad",
    )(*lefts, *rights)


def on_device(
    tokens,
    out_grad,
    routes,
    segments,
    capacity,
    attn_gain,
    w_qkv,
    query_gain,
    key_gain,
    w_out,
    ffn_gain,
    w_router,
    w_gate_up,
    w_down,
):
    n_expert = lax.axis_size("expert")
    n_shard = lax.axis_size("shard")
    rows, width = tokens.shape
    size = width // HEADS
    heads = HEADS // n_shard
    local_width = heads * size
    length = segments.shape[0]
    expert_count = capacity.shape[0]
    local_experts = w_down.shape[0]
    slots = rows * routes.shape[1] // expert_count
    shard_index = lax.axis_index("shard")
    expert_index = lax.axis_index("expert")
    source, behind = ring_place(n_expert)
    part_rows = w_qkv.shape[0]
    slice_rows = part_rows // n_expert
    relative = jnp.bitwise_xor(shard_index, jnp.arange(n_shard, dtype=jnp.int32))

    packed = jnp.concatenate(
        [attn_gain, ffn_gain, query_gain, key_gain, w_router.reshape(-1)]
    )
    packed = lax.all_to_all(
        jnp.broadcast_to(packed[None], (n_shard, packed.shape[0])), "shard", 0, 0, tiled=True
    )
    cuts = [part_rows, 2 * part_rows, 2 * part_rows + size // n_shard]
    cuts.append(cuts[-1] + size // n_shard)
    gain_one = packed[:, : cuts[0]].reshape(1, width).astype(F32)
    gain_two = packed[:, cuts[0] : cuts[1]].reshape(1, width).astype(F32)
    gain_query = packed[:, cuts[1] : cuts[2]].reshape(1, size).astype(F32)
    gain_key = packed[:, cuts[2] : cuts[3]].reshape(1, size).astype(F32)
    full_router = packed[:, cuts[3] :].reshape(width, expert_count)
    router_rows = full_router.T

    own_slice = lax.dynamic_slice_in_dim(w_qkv, expert_index * slice_rows, slice_rows)
    own_slice = own_slice.reshape(slice_rows, 3, n_shard, local_width).transpose(2, 0, 1, 3)
    own_slice = lax.all_to_all(
        own_slice.reshape(n_shard, slice_rows, 3 * local_width), "shard", 0, 0, tiled=True
    )
    own_slice = own_slice.reshape(n_shard * slice_rows, 3 * local_width)

    ahead, back = ring_perms(n_expert)
    dy_first = (
        lax.ppermute(out_grad, "expert", ahead),
        lax.ppermute(out_grad, "expert", back),
    )
    w_blocks = ring_gather(tied(own_slice, dy_first), n_expert)
    w_local = jnp.zeros((n_shard, n_expert, slice_rows, 3 * local_width), BF16)
    for r in arrivals(n_expert):
        w_local = lax.dynamic_update_slice(
            w_local,
            w_blocks[r].reshape(n_shard, 1, slice_rows, 3 * local_width),
            (0, source[r], 0, 0),
        )
    w_local = w_local.reshape(width, 3 * local_width)

    token_parts = shard_gather(tied(tokens, own_slice))
    token_blocks = jnp.concatenate(token_parts, axis=0)

    routes_all = lax.all_to_all(
        jnp.broadcast_to(routes[None], (n_expert,) + routes.shape), "expert", 0, 0, tiled=True
    )[source]

    gate_own, up_own = w_gate_up[:, 0], w_gate_up[:, 1]
    gate_parts = shard_gather(tied(gate_own, token_parts[2]))
    up_parts = shard_gather(tied(up_own, gate_parts[2]))
    gate_full, up_full = jnp.stack(gate_parts), jnp.stack(up_parts)

    my_experts = expert_index * local_experts + jnp.arange(local_experts, dtype=jnp.int32)
    named = jnp.any(
        routes_all[None, :, :, :] == my_experts[:, None, None, None], axis=3
    )
    order = jnp.arange(rows, dtype=jnp.int32)
    before = (order[:, None] < order[None, :]).astype(BF16)
    earlier = jnp.einsum(
        "ebu,ut->ebt", named.astype(BF16), before, preferred_element_type=F32
    ).astype(jnp.int32)
    my_limits = lax.dynamic_slice_in_dim(capacity, expert_index * local_experts, local_experts)
    slot_of = jnp.where(named & (earlier < my_limits[:, None, None]), earlier, -1)

    position = (
        relative[:, None] * rows + jnp.arange(rows, dtype=jnp.int32)[None, :]
    ).reshape(-1).astype(F32)
    half_size = size // 2
    frequency = THETA ** (-(2.0 * jnp.arange(half_size, dtype=F32)) / size)
    angles = position[:, None] * frequency[None, :]
    cosines, sines = jnp.cos(angles), jnp.sin(angles)
    docs = segments.reshape(n_shard, rows)[relative].reshape(-1)
    tables = (
        jnp.concatenate([cosines, cosines], axis=1),
        jnp.concatenate([-sines, sines], axis=1),
        docs[:, None],
        docs[None, :],
        gain_query,
        gain_key,
    )

    token_float = token_blocks.astype(F32)
    scale_one = rms_scale(token_float)
    normed = (token_float * scale_one * gain_one).astype(BF16)
    qkv_pre = jnp.dot(normed, w_local, preferred_element_type=F32)
    mixed = attention(qkv_pre, tables, heads, size)
    dy_blocks = ring_rest(
        out_grad, dy_first, n_expert, {2: w_blocks[n_expert // 2], 3: mixed}
    )
    attended = jnp.dot(tied(mixed, dy_blocks[2]), w_out, preferred_element_type=F32).astype(BF16)
    own_tokens = tokens.astype(F32)
    hidden = own_tokens + shard_scatter(list(attended.reshape(n_shard, rows, width)))
    scale_two = rms_scale(hidden)
    ffn_low = (hidden * scale_two * gain_two).astype(BF16)
    router = jax.nn.softmax(
        jnp.dot(ffn_low, full_router, preferred_element_type=F32), axis=-1
    )
    down_full = jnp.stack(shard_gather(tied(w_down, up_parts[2])))

    ffn_blocks = ring_gather(tied(ffn_low, dy_blocks[3]), n_expert)
    groups = block_groups(n_expert)
    base = (expert_index * local_experts).reshape(1).astype(jnp.int32)
    results, slot_groups = [], []
    for group in groups:
        slots_g = jnp.stack([slot_of[:, r] for r in group], axis=1)
        if results:
            slots_g = tied(slots_g, results[-1][-1])
        slot_groups.append(slots_g)
        results.append(
            expert_group(
                base,
                [ffn_blocks[r] for r in group],
                [dy_blocks[r] for r in group],
                slot_groups[-1],
                router_rows,
                gate_full,
                up_full,
                down_full,
                slots,
            )
        )
    rows_in, rows_cot, act, gate_back, up_back, terms, router_terms = map(list, zip(*results))
    where_is = {r: (g, i) for g, group in enumerate(groups) for i, r in enumerate(group)}

    def picker(arrays):
        return lambda r: arrays[where_is[r][0]][where_is[r][1]]

    ffn_back, hops = ring_scatter(picker(terms), n_expert)
    back_to = jnp.stack(
        [router_terms[where_is[r][0]][:, where_is[r][1]] for r in range(n_expert)]
    )
    router_back = lax.all_to_all(
        back_to[behind], "expert", split_axis=0, concat_axis=0, tiled=True
    ).reshape(expert_count, rows).T

    gate_parts = expert_grad(rows_in, gate_back, n_shard)
    up_parts = expert_grad(tied(rows_in, hops[0]), up_back, n_shard)
    up_grads = shard_scatter(list(up_parts))
    down_parts = expert_grad(tied(act, hops[1]), rows_cot, n_shard)
    out_terms = [
        expert_output(slots_g, tied(act_g, hops[2]), down_full)
        for slots_g, act_g in zip(slot_groups, act)
    ]
    farthest = where_is[n_expert // 2][0]
    out_terms[farthest] = tied(out_terms[farthest], ffn_back)
    out_sum, out_hops = ring_scatter(picker(out_terms), n_expert)
    layer_out = (hidden + out_sum).astype(BF16)

    logit_back = (
        router * (router_back - jnp.sum(router * router_back, axis=-1, keepdims=True))
    ).astype(BF16)
    router_grad = dot_f32(ffn_low, logit_back, ((0,), (0,)))
    ffn_back = ffn_back + dot_f32(logit_back, full_router, ((1,), (1,)))
    gain_two_part = jnp.sum(ffn_back * hidden * scale_two, axis=0)
    hidden_back = out_grad.astype(F32) + norm_back(ffn_back, hidden, scale_two, gain_two)

    mix_back = jnp.concatenate(shard_gather(hidden_back.astype(BF16)), axis=0)
    gate_grads, far = shard_scatter_late(list(gate_parts), mix_back)
    up_grads, far = shard_scatter_late(list(up_parts), far)
    down_grad, far = shard_scatter_late(list(down_parts), far)
    head_back = dot_f32(mix_back, w_out, ((1,), (1,))).astype(BF16)
    out_part = dot_f32(mixed, mix_back, ((0,), (0,))).astype(BF16)
    query_back, key_back, value_back, head_gains = attention_back(
        qkv_pre, head_back, tables, heads, size
    )
    qkv_back = jnp.concatenate([query_back, key_back, value_back], axis=1)
    qkv_part = dot_f32(normed, qkv_back, ((0,), (0,))).astype(BF16)
    normed_back = dot_f32(tied(qkv_back, qkv_part), w_local, ((1,), (1,)))
    gain_one_part = jnp.sum(normed_back * token_float * scale_one, axis=0)
    own_back = shard_scatter(list(normed_back.astype(BF16).reshape(n_shard, rows, width)))
    tokens_grad = hidden_back + norm_back(own_back, own_tokens, scale_one[:rows], gain_one)

    def placed_blocks(blocks):
        total = jnp.zeros((n_expert * blocks[0].shape[0], blocks[0].shape[1]), F32)
        for r in arrivals(n_expert):
            total = lax.dynamic_update_slice(
                total, blocks[r].astype(F32), (source[r] * blocks[r].shape[0], 0)
            )
        return total

    out_terms_w = out_part.reshape(n_expert, slice_rows, width)
    out_mine, _ = ring_scatter(
        lambda r: lax.dynamic_index_in_dim(out_terms_w, source[r], 0, keepdims=False), n_expert
    )
    out_total = placed_blocks(ring_gather(out_mine.astype(BF16), n_expert))
    qkv_terms = qkv_part.reshape(n_shard, n_expert, slice_rows, 3 * local_width)
    qkv_mine, _ = ring_scatter(
        lambda r: lax.dynamic_index_in_dim(qkv_terms, source[r], 1, keepdims=False).reshape(
            n_shard * slice_rows, 3 * local_width
        ),
        n_expert,
    )
    qkv_mine = lax.all_to_all(
        qkv_mine.astype(BF16), "shard", split_axis=0, concat_axis=0, tiled=True
    )
    qkv_mine = (
        qkv_mine.reshape(n_shard, slice_rows, 3, local_width)
        .transpose(1, 2, 0, 3)
        .reshape(slice_rows, 3 * width)
    )
    qkv_total = placed_blocks(ring_gather(qkv_mine, n_expert))

    small = jnp.concatenate(
        [
            gain_one_part.reshape(n_shard, -1),
            gain_two_part.reshape(n_shard, -1),
            head_gains[0].reshape(n_shard, -1),
            head_gains[1].reshape(n_shard, -1),
            router_grad.reshape(n_shard, -1),
        ],
        axis=1,
    )
    small = lax.all_to_all(small, "shard", split_axis=0, concat_axis=0, tiled=True)
    small = tree_sum(jnp.sum(small, axis=0).reshape(1, -1), "expert")[0]
    gate_up_grad = jnp.stack([gate_grads, up_grads], axis=1)
    return (
        layer_out,
        tokens_grad,
        small[: cuts[0]],
        qkv_total,
        small[cuts[1] : cuts[2]],
        small[cuts[2] : cuts[3]],
        out_total,
        small[cuts[0] : cuts[1]],
        small[cuts[3] :].reshape(part_rows, expert_count),
        gate_up_grad,
        down_grad,
    )


def solution(mesh):
    placed = (
        P(("expert", "shard"), None),
        P(("expert", "shard"), None),
        P(("expert", "shard"), None),
        P("expert"),
        P(),
        P("shard"),
        P("shard", None),
        P("shard"),
        P("shard"),
        P("shard", None),
        P("shard"),
        P("shard", None),
        P("expert", None, None, "shard"),
        P("expert", "shard", None),
    )
    return jax.shard_map(
        on_device,
        mesh=mesh,
        in_specs=placed,
        out_specs=(
            P(("expert", "shard"), None),
            P(("expert", "shard"), None),
            P("shard"),
            P("shard", None),
            P("shard"),
            P("shard"),
            P("shard", None),
            P("shard"),
            P("shard", None),
            P("expert", None, None, "shard"),
            P("expert", "shard", None),
        ),
        check_vma=False,
    )
```

```python
import functools

import jax
import jax.numpy as jnp
from jax import lax
from jax.experimental import pallas as pl
from jax.experimental.pallas import tpu as pltpu
from jax.sharding import PartitionSpec as P

HEADS = 16
EPS = 1e-06
THETA = 50000.0
NEG_BIG = -1e30
F32 = jnp.float32
BF16 = jnp.bfloat16


def dot_f32(left, right, dims):
    return lax.dot_general(left, right, (dims, ((), ())), preferred_element_type=F32)


def rms_scale(values):
    return lax.rsqrt(jnp.mean(values * values, axis=-1, keepdims=True) + EPS)


def norm_back(grad_in, values, scale, gain):
    weighted = grad_in * gain
    return scale * weighted - values * scale**3 * jnp.mean(
        weighted * values, axis=-1, keepdims=True
    )


def ring_order(size):
    if size == 8:
        return [0, 2, 4, 6, 7, 5, 3, 1]
    return list(range(size))


def ring_perms(size):
    order = ring_order(size)
    ahead = [(order[i], order[(i + 1) % size]) for i in range(size)]
    return ahead, [(b, a) for a, b in ahead]


def ring_place(size):
    order = ring_order(size)
    places = [0] * size
    for place, index in enumerate(order):
        places[index] = place
    mine = jnp.array(places, jnp.int32)[lax.axis_index("expert")]
    source = jnp.array(order, jnp.int32)[
        jnp.mod(mine - jnp.arange(size, dtype=jnp.int32), size)
    ]
    behind = jnp.mod(mine - jnp.array(places, jnp.int32), size)
    return source, behind


def tied(value, *others):
    return lax.optimization_barrier((value, others))[0]


def zero_of(*others):
    total = jnp.zeros((), F32)
    for other in jax.tree.leaves(others):
        total = total + jnp.minimum(jnp.abs(other[(0,) * other.ndim].astype(F32)), 0.0)
    return total


def held(value, *others):
    return value + zero_of(*others).astype(value.dtype)


def ring_gather(block, size, whole=True):
    ahead, back = ring_perms(size)
    first = (lax.ppermute(block, "expert", ahead), lax.ppermute(block, "expert", back))
    return ring_rest(block, first, size, {}, whole)


def ring_rest(block, first, size, gates, whole=True):
    ahead, back = ring_perms(size)
    blocks = [block] * size
    from_behind, from_ahead = first
    blocks[1], blocks[size - 1] = first
    for step in range(2, size // 2):
        if step in gates:
            from_behind, from_ahead = tied((from_behind, from_ahead), gates[step])
        from_behind = lax.ppermute(from_behind, "expert", ahead)
        from_ahead = lax.ppermute(from_ahead, "expert", back)
        blocks[step] = from_behind
        blocks[size - step] = from_ahead
    if whole:
        ring_last(blocks, size)
    return blocks


def ring_last(blocks, size, after=()):
    ahead, back = ring_perms(size)
    half = blocks[0].shape[0] // 2
    top, bottom = blocks[size // 2 - 1][:half], blocks[size // 2 + 1][half:]
    if after:
        top, bottom = held(top, after), held(bottom, after)
    blocks[size // 2] = jnp.concatenate(
        [lax.ppermute(top, "expert", ahead), lax.ppermute(bottom, "expert", back)], axis=0
    )


def arrivals(size):
    order = [0]
    for step in range(1, size // 2):
        order += [step, size - step]
    return order + [size // 2]


def ring_scatter(pick, size, after=(), brought=None):
    ahead, back = ring_perms(size)
    first = pick(size // 2)
    if after:
        first = held(first, after)
    half = first.shape[0] // 2
    down = lax.ppermute(first[:half].astype(BF16), "expert", back)
    up = lax.ppermute(first[half:].astype(BF16), "expert", ahead)
    hops = [] if brought is None else brought
    hops.append(down)
    for step in range(size // 2 - 1, 0, -1):
        own_down, own_up = pick(step).astype(F32), pick(size - step).astype(F32)
        if step == size // 2 - 1:
            zeros = jnp.zeros_like(down)
            down = jnp.concatenate([down, zeros], axis=0)
            up = jnp.concatenate([zeros, up], axis=0)
        both = zero_of(down, up)
        down, up = (
            lax.ppermute((own_down + down.astype(F32) + both).astype(BF16), "expert", back),
            lax.ppermute((own_up + up.astype(F32) + both).astype(BF16), "expert", ahead),
        )
        hops.append(down)
    return pick(0).astype(F32) + down.astype(F32) + up.astype(F32), hops


def swap(value, bit):
    size = lax.axis_size("shard")
    return lax.ppermute(value, "shard", [(i, i ^ bit) for i in range(size)])


def shard_gather(block):
    far = swap(block, 2)
    near = swap(block, 1)
    return [block, near, far, swap(far, 1)]


def shard_scatter(blocks):
    near = [swap(blocks[3].astype(BF16), 1), swap(blocks[1].astype(BF16), 1)]
    far = swap((blocks[2].astype(F32) + near[0].astype(F32)).astype(BF16), 2)
    return blocks[0].astype(F32) + near[1].astype(F32) + far.astype(F32)


def tree_sum(value, axis):
    size = lax.axis_size(axis)
    bit = 1
    while bit < size:
        value = value + lax.ppermute(value, axis, [(i, i ^ bit) for i in range(size)])
        bit *= 2
    return value


def turned(values, cosines, sines):
    return values * cosines + pltpu.roll(values, values.shape[-1] // 2, 1) * sines


def attention_kernel(scale, chunk, q_ref, k_ref, v_ref, cos_ref, sin_ref, col_ref, row_ref, gq_ref, gk_ref, out_ref):
    cosines, sines = cos_ref[...], sin_ref[...]
    q_pre, k_pre = q_ref[...], k_ref[...]
    query = turned(q_pre * rms_scale(q_pre) * gq_ref[...], cosines, sines).astype(BF16)
    key = turned(k_pre * rms_scale(k_pre) * gk_ref[...], cosines, sines).astype(BF16)
    value = v_ref[...].astype(BF16)
    docs = row_ref[...]
    for start in range(0, q_pre.shape[0], chunk):
        rows = slice(start, start + chunk)
        scores = dot_f32(query[rows], key, ((1,), (1,))) * scale
        scores = jnp.where(col_ref[rows, :] == docs, scores, NEG_BIG)
        shifted = jnp.exp(scores - jnp.max(scores, axis=-1, keepdims=True))
        probs = shifted * (1.0 / jnp.sum(shifted, axis=-1, keepdims=True))
        out_ref[rows, :] = dot_f32(probs.astype(BF16), value, ((1,), (0,))).astype(BF16)


def attention_back_kernel(
    scale, chunk, q_ref, k_ref, v_ref, do_ref, cos_ref, sin_ref, col_ref, row_ref, gq_ref, gk_ref,
    dq_ref, dk_ref, dv_ref, gains_ref, dq_acc, dk_acc, dv_acc,
):
    cosines, sines = cos_ref[...], sin_ref[...]
    q_pre, k_pre = q_ref[...], k_ref[...]
    q_scale, k_scale = rms_scale(q_pre), rms_scale(k_pre)
    query = turned(q_pre * q_scale * gq_ref[...], cosines, sines).astype(BF16)
    key = turned(k_pre * k_scale * gk_ref[...], cosines, sines).astype(BF16)
    value = v_ref[...].astype(BF16)
    docs = row_ref[...]
    for start in range(0, q_pre.shape[0], chunk):
        rows = slice(start, start + chunk)
        out_back = do_ref[rows, :]
        scores = dot_f32(query[rows], key, ((1,), (1,))) * scale
        scores = jnp.where(col_ref[rows, :] == docs, scores, NEG_BIG)
        shifted = jnp.exp(scores - jnp.max(scores, axis=-1, keepdims=True))
        probs = shifted * (1.0 / jnp.sum(shifted, axis=-1, keepdims=True))
        prob_back = dot_f32(out_back, value, ((1,), (1,)))
        score_back = (
            probs * (prob_back - jnp.sum(probs * prob_back, axis=-1, keepdims=True))
        ).astype(BF16)
        dq_acc[rows, :] = dot_f32(score_back, key, ((1,), (0,)))
        dk_part = dot_f32(score_back, query[rows], ((0,), (0,)))
        dv_part = dot_f32(probs.astype(BF16), out_back, ((0,), (0,)))
        if start == 0:
            dk_acc[...] = dk_part
            dv_acc[...] = dv_part
        else:
            dk_acc[...] += dk_part
            dv_acc[...] += dv_part
    dv_ref[...] = dv_acc[...].astype(BF16)

    @pl.when(pl.program_id(0) == 0)
    def _():
        gains_ref[...] = jnp.zeros_like(gains_ref)

    for place, (acc, pre, pre_scale, gain, out) in enumerate(
        (
            (dq_acc, q_pre, q_scale, gq_ref[...], dq_ref),
            (dk_acc, k_pre, k_scale, gk_ref[...], dk_ref),
        )
    ):
        grad = turned((acc[...] * scale).astype(BF16).astype(F32), cosines, -sines)
        gains_ref[place : place + 1, :] += jnp.sum(grad * pre * pre_scale, axis=0, keepdims=True)
        out[...] = norm_back(grad, pre, pre_scale, gain).astype(BF16)


def attention_specs(length, size, heads, first=0):
    def column(part):
        return pl.BlockSpec((length, size), lambda h: (0, part * heads + first + h))

    def whole(*shape):
        return pl.BlockSpec(shape, lambda h: (0, 0))

    pre = [column(0), column(1), column(2)]
    rest = [
        whole(length, size),
        whole(length, size),
        whole(length, 1),
        whole(1, length),
        whole(1, size),
        whole(1, size),
    ]
    return column(0), pre, rest


def attention(qkv_pre, tables, heads, size):
    length = qkv_pre.shape[0]
    own, pre, rest = attention_specs(length, size, heads)
    return pl.pallas_call(
        functools.partial(attention_kernel, size**-0.5, min(256, length)),
        grid=(heads,),
        in_specs=pre + rest,
        out_specs=own,
        out_shape=jax.ShapeDtypeStruct((length, heads * size), BF16),
        cost_estimate=pl.CostEstimate(
            flops=4 * heads * length * length * size,
            bytes_accessed=qkv_pre.size * 4 + length * heads * size * 2,
            transcendentals=heads * length * length,
        ),
        name="attention",
    )(qkv_pre, qkv_pre, qkv_pre, *tables)


def attention_back(qkv_pre, head_back, tables, heads, size, first, count):
    length = qkv_pre.shape[0]
    given, pre, rest = attention_specs(length, size, heads, first)
    own = pl.BlockSpec((length, size), lambda h: (0, h))
    shape = jax.ShapeDtypeStruct((length, count * size), BF16)
    return pl.pallas_call(
        functools.partial(attention_back_kernel, size**-0.5, min(256, length)),
        grid=(count,),
        in_specs=pre + [given] + rest,
        out_specs=[own, own, own, pl.BlockSpec((2, size), lambda h: (0, 0))],
        out_shape=[shape, shape, shape, jax.ShapeDtypeStruct((2, size), F32)],
        scratch_shapes=[pltpu.VMEM((length, size), F32)] * 3,
        cost_estimate=pl.CostEstimate(
            flops=10 * count * length * length * size,
            bytes_accessed=qkv_pre.size * 4 + 4 * length * count * size * 2,
            transcendentals=heads * length * length,
        ),
        name="attention_back",
    )(qkv_pre, qkv_pre, qkv_pre, head_back, *tables)


GROUP = 4
ATTENTION_PARTS = 1


def block_groups(size):
    if size == 8:
        return [[0, 1, 7], [2, 6], [4, 3, 5]]
    order = arrivals(size)
    return [order[i : i + GROUP] for i in range(0, size, GROUP)]


VMEM_BYTES = 60 * 1024 * 1024


def expert_kernel(count, extras, base_ref, *refs):
    refs = refs[extras:]
    x_refs, dy_refs = refs[:count], refs[count : 2 * count]
    slot_ref, router_ref, wg_ref, wu_ref, wd_ref = refs[2 * count : 2 * count + 5]
    rin_ref, rcot_ref, act_ref, gb_ref, ub_ref, rback_ref = refs[
        2 * count + 5 : 2 * count + 11
    ]
    weight_ref, gg_ref = refs[2 * count + 11 :]
    expert, part = pl.program_id(0), pl.program_id(1)
    tokens = x_refs[0].shape[0]
    slots = rin_ref.shape[1] // count

    def pick_of(block):
        places = lax.broadcasted_iota(jnp.int32, (slots, tokens), 0)
        return places == slot_ref[0, block : block + 1, :]

    def low(mask):
        return jnp.where(mask, 1.0, 0.0).astype(BF16)

    @pl.when(part == 0)
    def _():
        mine = base_ref[0] + expert
        for block in range(count):
            rows = pl.ds(block * slots, slots)
            pick = pick_of(block)
            pick_low = low(pick)
            x_block = x_refs[block][...]
            rin_ref[0, rows, :] = dot_f32(pick_low, x_block, ((1,), (0,))).astype(BF16)
            rcot_ref[0, rows, :] = dot_f32(
                pick_low, dy_refs[block][...], ((1,), (0,))
            ).astype(BF16)
            logits = dot_f32(router_ref[...], x_block, ((1,), (1,)))
            powers = jnp.exp(logits - jnp.max(logits, axis=0, keepdims=True))
            router = powers / jnp.sum(powers, axis=0, keepdims=True)
            which = lax.broadcasted_iota(jnp.int32, router.shape, 0)
            gate = jnp.sum(jnp.where(which == mine, router, 0.0), axis=0, keepdims=True)
            weight_ref[rows, :] = jnp.sum(
                jnp.where(pick, gate, 0.0), axis=1, keepdims=True
            )

    rows_in, rows_cot = rin_ref[0], rcot_ref[0]
    w_gate, w_up, w_back = wg_ref[0, 0, 0], wu_ref[0, 0, 0], wd_ref[0, 0]
    weight = weight_ref[...]
    pre_gate = dot_f32(rows_in, w_gate, ((1,), (0,)))
    pre_up = dot_f32(rows_in, w_up, ((1,), (0,)))
    cot_down = dot_f32(rows_cot, w_back, ((1,), (1,)))
    sigmoid = jax.nn.sigmoid(pre_gate)
    silu = pre_gate * sigmoid
    act = silu * pre_up
    share = act * cot_down
    folded = share[:, :128]
    for lane in range(128, share.shape[1], 128):
        folded = folded + share[:, lane : lane + 128]
    act_back = weight * cot_down
    act_ref[0] = (weight * act).astype(BF16)
    gb_ref[0] = (act_back * pre_up * (sigmoid + silu * (1.0 - sigmoid))).astype(BF16)
    ub_ref[0] = (act_back * silu).astype(BF16)

    @pl.when(part == 0)
    def _():
        gg_ref[...] = folded

    @pl.when(part > 0)
    def _():
        gg_ref[...] += folded

    @pl.when(part == pl.num_programs(1) - 1)
    def _():
        for block in range(count):
            rows = pl.ds(block * slots, slots)
            pick = pick_of(block)
            share = jnp.sum(gg_ref[rows, :], axis=1, keepdims=True)
            rback_ref[0, block : block + 1, :] = jnp.sum(
                jnp.where(pick, share, 0.0), axis=0, keepdims=True
            )


def weight_spec(shape, which=None):
    if which is None:
        return pl.BlockSpec((1, 1) + shape[2:], lambda e, j: (j, e, 0, 0))
    return pl.BlockSpec((1, 1, 1) + shape[3:], lambda e, j: (j, e, which, 0, 0))


def expert_group(base, x_blocks, dy_blocks, slot_of, router_rows, w_gate_up, w_down, slots, after):
    count = len(x_blocks)
    tokens, width = x_blocks[0].shape
    parts, experts, hidden = w_down.shape[:3]
    rows = count * slots

    def still(shape):
        return pl.BlockSpec(
            shape, lambda e, j: (0,) * len(shape), pipeline_mode=pl.Buffered(1)
        )

    def per_expert(*shape):
        return pl.BlockSpec((1,) + shape, lambda e, j: (e, 0, 0))

    part = pl.BlockSpec((1, rows, hidden), lambda e, j: (e, 0, j))
    wide = jax.ShapeDtypeStruct((experts, rows, width), BF16)
    deep = jax.ShapeDtypeStruct((experts, rows, parts * hidden), BF16)
    flops = 6 * rows * width * parts * hidden * experts
    return pl.pallas_call(
        functools.partial(expert_kernel, count, len(after)),
        grid=(experts, parts),
        in_specs=[pl.BlockSpec(memory_space=pltpu.SMEM)]
        + [pl.BlockSpec(memory_space=pl.ANY)] * len(after)
        + [still((tokens, width))] * (2 * count)
        + [
            per_expert(count, tokens),
            still(router_rows.shape),
            weight_spec(w_gate_up.shape, 0),
            weight_spec(w_gate_up.shape, 1),
            weight_spec(w_down.shape),
        ],
        out_specs=[
            per_expert(rows, width),
            per_expert(rows, width),
            part,
            part,
            part,
            per_expert(count, tokens),
        ],
        out_shape=[
            wide,
            wide,
            deep,
            deep,
            deep,
            jax.ShapeDtypeStruct((experts, count, tokens), F32),
        ],
        scratch_shapes=[
            pltpu.VMEM((rows, 1), F32),
            pltpu.VMEM((rows, 128), F32),
        ],
        compiler_params=pltpu.CompilerParams(vmem_limit_bytes=VMEM_BYTES),
        cost_estimate=pl.CostEstimate(
            flops=flops, bytes_accessed=3 * w_gate_up.size, transcendentals=rows * parts * hidden
        ),
        name="experts",
    )(base, *after, *x_blocks, *dy_blocks, slot_of, router_rows, w_gate_up, w_gate_up, w_down)


def combine_kernel(count, pairs, dim, slot_ref, *refs):
    lefts, weights = refs[:pairs], refs[pairs : 2 * pairs]
    terms_ref, acc_ref, sum_ref = refs[-3:]
    expert, part = pl.program_id(0), pl.program_id(1)
    tokens = terms_ref.shape[1]
    slots = acc_ref.shape[0] // count
    out = None
    for left, weight in zip(lefts, weights):
        matrix = weight[(0,) * (len(weight.shape) - 2)]
        product = dot_f32(left[0], matrix, ((1,), (dim,)))
        out = product if out is None else out + product

    @pl.when(part == 0)
    def _():
        acc_ref[...] = out

    @pl.when(part > 0)
    def _():
        acc_ref[...] += out

    @pl.when(part == pl.num_programs(1) - 1)
    def _():
        for block in range(count):
            places = lax.broadcasted_iota(jnp.int32, (slots, tokens), 0)
            pick = jnp.where(places == slot_ref[0, block : block + 1, :], 1.0, 0.0).astype(BF16)
            rows = acc_ref[pl.ds(block * slots, slots), :].astype(BF16)
            term = dot_f32(pick, rows, ((0,), (0,)))

            @pl.when(expert == 0)
            def _():
                sum_ref[block] = term

            @pl.when(expert > 0)
            def _():
                sum_ref[block] += term

            @pl.when(expert == pl.num_programs(0) - 1)
            def _():
                terms_ref[block] = sum_ref[block].astype(BF16)


def expert_combine(slot_of, lefts, weight, dim, after):
    experts, count, tokens = slot_of.shape
    parts = weight.shape[0]
    hidden, width = weight.shape[-2:] if dim == 0 else weight.shape[-1:-3:-1]
    rows = lefts[0].shape[1]
    pairs = len(lefts)
    which = range(pairs) if pairs > 1 else [None]
    return pl.pallas_call(
        functools.partial(combine_kernel, count, pairs, dim),
        grid=(experts, parts),
        in_specs=[pl.BlockSpec((1, count, tokens), lambda e, j: (e, 0, 0))]
        + [pl.BlockSpec((1, rows, hidden), lambda e, j: (e, 0, j))] * pairs
        + [weight_spec(weight.shape, place) for place in which]
        + [pl.BlockSpec(memory_space=pl.ANY)] * len(after),
        out_specs=pl.BlockSpec((count, tokens, width), lambda e, j: (0, 0, 0)),
        out_shape=jax.ShapeDtypeStruct((count, tokens, width), BF16),
        scratch_shapes=[
            pltpu.VMEM((rows, width), F32),
            pltpu.VMEM((count, tokens, width), F32),
        ],
        compiler_params=pltpu.CompilerParams(vmem_limit_bytes=VMEM_BYTES),
        cost_estimate=pl.CostEstimate(
            flops=2 * pairs * rows * width * parts * hidden * experts,
            bytes_accessed=2 * (weight.size + pairs * lefts[0].size + count * tokens * width),
            transcendentals=0,
        ),
        name="expert_combine",
    )(slot_of, *lefts, *[weight] * pairs, *after)


def grad_kernel(groups, *refs):
    total = None
    for left, right in zip(refs[:groups], refs[groups : 2 * groups]):
        part = dot_f32(left[0], right[0], ((0,), (0,)))
        total = part if total is None else total + part
    refs[-1][0, 0] = total.astype(BF16)


def expert_grad(lefts, rights, parts, after):
    experts = lefts[0].shape[0]
    hidden = min(lefts[0].shape[2], rights[0].shape[2]) // parts

    def spec(array, cut):
        width = hidden if cut else array.shape[2]
        return pl.BlockSpec(
            (1, array.shape[1], width), lambda e, j: (e, 0, j if cut else 0)
        )

    cut_left = lefts[0].shape[2] < rights[0].shape[2]
    shape = (
        hidden if cut_left else lefts[0].shape[2],
        rights[0].shape[2] if cut_left else hidden,
    )
    rows = sum(left.shape[1] for left in lefts)
    return pl.pallas_call(
        functools.partial(grad_kernel, len(lefts)),
        grid=(experts, parts),
        in_specs=[spec(left, cut_left) for left in lefts]
        + [spec(right, not cut_left) for right in rights]
        + [pl.BlockSpec(memory_space=pl.ANY)] * len(after),
        out_specs=pl.BlockSpec((1, 1) + shape, lambda e, j: (j, e, 0, 0)),
        out_shape=jax.ShapeDtypeStruct((parts, experts) + shape, BF16),
        compiler_params=pltpu.CompilerParams(vmem_limit_bytes=VMEM_BYTES),
        cost_estimate=pl.CostEstimate(
            flops=2 * rows * shape[0] * shape[1] * parts * experts,
            bytes_accessed=2 * experts * (parts * shape[0] * shape[1] + 3 * rows * shape[0]),
            transcendentals=0,
        ),
        name="expert_grad",
    )(*lefts, *rights, *after)


def on_device(
    tokens,
    out_grad,
    routes,
    segments,
    capacity,
    attn_gain,
    w_qkv,
    query_gain,
    key_gain,
    w_out,
    ffn_gain,
    w_router,
    w_gate_up,
    w_down,
):
    n_expert = lax.axis_size("expert")
    n_shard = lax.axis_size("shard")
    rows, width = tokens.shape
    size = width // HEADS
    heads = HEADS // n_shard
    local_width = heads * size
    length = segments.shape[0]
    expert_count = capacity.shape[0]
    local_experts = w_down.shape[0]
    slots = rows * routes.shape[1] // expert_count
    shard_index = lax.axis_index("shard")
    expert_index = lax.axis_index("expert")
    source, behind = ring_place(n_expert)
    part_rows = w_qkv.shape[0]
    slice_rows = part_rows // n_expert
    relative = jnp.bitwise_xor(shard_index, jnp.arange(n_shard, dtype=jnp.int32))

    packed = jnp.concatenate(
        [attn_gain, ffn_gain, query_gain, key_gain, w_router.reshape(-1)]
    )
    packed = lax.all_to_all(
        jnp.broadcast_to(packed[None], (n_shard, packed.shape[0])), "shard", 0, 0, tiled=True
    )
    cuts = [part_rows, 2 * part_rows, 2 * part_rows + size // n_shard]
    cuts.append(cuts[-1] + size // n_shard)
    gain_one = packed[:, : cuts[0]].reshape(1, width).astype(F32)
    gain_two = packed[:, cuts[0] : cuts[1]].reshape(1, width).astype(F32)
    gain_query = packed[:, cuts[1] : cuts[2]].reshape(1, size).astype(F32)
    gain_key = packed[:, cuts[2] : cuts[3]].reshape(1, size).astype(F32)
    full_router = packed[:, cuts[3] :].reshape(width, expert_count)
    router_rows = full_router.T

    own_slice = lax.dynamic_slice_in_dim(w_qkv, expert_index * slice_rows, slice_rows)
    own_slice = own_slice.reshape(slice_rows, 3, n_shard, local_width).transpose(2, 0, 1, 3)
    own_slice = lax.all_to_all(
        own_slice.reshape(n_shard, slice_rows, 3 * local_width), "shard", 0, 0, tiled=True
    )
    own_slice = own_slice.reshape(n_shard * slice_rows, 3 * local_width)

    ahead, back = ring_perms(n_expert)
    dy_first = (
        lax.ppermute(out_grad, "expert", ahead),
        lax.ppermute(out_grad, "expert", back),
    )
    w_blocks = ring_gather(tied(own_slice, dy_first), n_expert)
    w_local = jnp.zeros((n_shard, n_expert, slice_rows, 3 * local_width), BF16)
    for r in arrivals(n_expert):
        w_local = lax.dynamic_update_slice(
            w_local,
            w_blocks[r].reshape(n_shard, 1, slice_rows, 3 * local_width),
            (0, source[r], 0, 0),
        )
    w_local = w_local.reshape(width, 3 * local_width)

    token_parts = shard_gather(tied(tokens, own_slice))
    token_blocks = jnp.concatenate(token_parts, axis=0)

    routes_all = lax.all_to_all(
        jnp.broadcast_to(routes[None], (n_expert,) + routes.shape), "expert", 0, 0, tiled=True
    )[source]

    gate_up_full = lax.all_gather(w_gate_up, "shard")
    down_full = lax.all_gather(w_down, "shard")

    my_experts = expert_index * local_experts + jnp.arange(local_experts, dtype=jnp.int32)
    named = jnp.any(
        routes_all[None, :, :, :] == my_experts[:, None, None, None], axis=3
    )
    order = jnp.arange(rows, dtype=jnp.int32)
    before = (order[:, None] < order[None, :]).astype(BF16)
    earlier = jnp.einsum(
        "ebu,ut->ebt", named.astype(BF16), before, preferred_element_type=F32
    ).astype(jnp.int32)
    my_limits = lax.dynamic_slice_in_dim(capacity, expert_index * local_experts, local_experts)
    slot_of = jnp.where(named & (earlier < my_limits[:, None, None]), earlier, -1)

    position = (
        relative[:, None] * rows + jnp.arange(rows, dtype=jnp.int32)[None, :]
    ).reshape(-1).astype(F32)
    half_size = size // 2
    frequency = THETA ** (-(2.0 * jnp.arange(half_size, dtype=F32)) / size)
    angles = position[:, None] * frequency[None, :]
    cosines, sines = jnp.cos(angles), jnp.sin(angles)
    docs = segments.reshape(n_shard, rows)[relative].reshape(-1)
    tables = (
        jnp.concatenate([cosines, cosines], axis=1),
        jnp.concatenate([-sines, sines], axis=1),
        docs[:, None],
        docs[None, :],
        gain_query,
        gain_key,
    )

    token_float = token_blocks.astype(F32)
    scale_one = rms_scale(token_float)
    normed = (token_float * scale_one * gain_one).astype(BF16)
    qkv_pre = jnp.dot(normed, w_local, preferred_element_type=F32)
    mixed = attention(qkv_pre, tables, heads, size)
    dy_blocks = ring_rest(
        out_grad, dy_first, n_expert, {2: w_blocks[n_expert // 2], 3: mixed}
    )
    attended = jnp.dot(tied(mixed, dy_blocks[2]), w_out, preferred_element_type=F32).astype(BF16)
    own_tokens = tokens.astype(F32)
    hidden = own_tokens + shard_scatter(list(attended.reshape(n_shard, rows, width)))
    scale_two = rms_scale(hidden)
    ffn_low = (
        hidden * scale_two * gain_two
        + zero_of(dy_blocks[n_expert // 2 - 1], dy_blocks[n_expert // 2 + 1])
    ).astype(BF16)
    router = jax.nn.softmax(
        jnp.dot(ffn_low, full_router, preferred_element_type=F32), axis=-1
    )

    ffn_blocks = ring_gather(tied(ffn_low, dy_blocks[3]), n_expert, whole=False)
    groups = block_groups(n_expert)
    base = (expert_index * local_experts).reshape(1).astype(jnp.int32)
    results, slot_groups = [], []
    for group in groups:
        slots_g = jnp.stack([slot_of[:, r] for r in group], axis=1)
        if n_expert // 2 in group:
            ring_last(ffn_blocks, n_expert, [results[0][-1]] if results else ())
        slot_groups.append(slots_g)
        results.append(
            expert_group(
                base,
                [ffn_blocks[r] for r in group],
                [dy_blocks[r] for r in group],
                slot_groups[-1],
                router_rows,
                gate_up_full,
                down_full,
                slots,
                [results[-1][-1]] if results else [],
            )
        )
    rows_in, rows_cot, act, gate_back, up_back, router_terms = map(list, zip(*results))
    where_is = {r: (g, i) for g, group in enumerate(groups) for i, r in enumerate(group)}

    def picker(arrays):
        return lambda r: arrays[where_is[r][0]][where_is[r][1]]

    out_terms, terms = [None] * len(groups), [None] * len(groups)
    latest = router_terms[-1]
    last = len(groups) - 1
    out_hops = []

    def pick_out(r):
        g, place_in = where_is[r]
        if out_terms[g] is None:
            after = [out_terms[g + 1]] if g < last else [router_terms[-1]]
            after += out_hops[:1] if g == 0 else []
            out_terms[g] = expert_combine(slot_groups[g], [act[g]], down_full, 0, after)
        return out_terms[g][place_in]

    for g in range(last, 0, -1):
        pick_out(groups[g][0])
    out_sum, _ = ring_scatter(pick_out, n_expert, brought=out_hops)
    layer_out = (hidden + out_sum).astype(BF16)
    latest = out_terms[0]
    for g in range(last, -1, -1):
        latest = terms[g] = expert_combine(
            slot_groups[g],
            [gate_back[g], up_back[g]],
            gate_up_full,
            1,
            [latest] + (out_hops[1:2] if g == last - 1 else []),
        )
    back_hops = []
    ffn_back, _ = ring_scatter(picker(terms), n_expert, after=out_hops[2:3], brought=back_hops)
    back_to = jnp.stack(
        [router_terms[where_is[r][0]][:, where_is[r][1]] for r in range(n_expert)]
    )
    router_back = lax.all_to_all(
        back_to[behind], "expert", split_axis=0, concat_axis=0, tiled=True
    ).reshape(expert_count, rows).T

    gate_parts = expert_grad(rows_in, gate_back, n_shard, [latest] + out_hops[2:3])
    up_parts = expert_grad(rows_in, up_back, n_shard, [gate_parts] + back_hops[:1])
    ffn_back = ffn_back + zero_of(up_parts)

    logit_back = (
        router * (router_back - jnp.sum(router * router_back, axis=-1, keepdims=True))
    ).astype(BF16)
    router_grad = dot_f32(ffn_low, logit_back, ((0,), (0,)))
    ffn_back = ffn_back + dot_f32(logit_back, full_router, ((1,), (1,)))
    gain_two_part = jnp.sum(ffn_back * hidden * scale_two, axis=0)
    hidden_back = out_grad.astype(F32) + norm_back(ffn_back, hidden, scale_two, gain_two)

    hidden_low = hidden_back.astype(BF16)
    mix_parts = shard_gather(hidden_low)
    mix_back = jnp.concatenate(mix_parts, axis=0)

    def to_owners(parts):
        return lax.psum_scatter(
            parts.reshape((n_shard * local_experts,) + parts.shape[2:]),
            "shard",
            scatter_dimension=0,
            tiled=True,
        )

    gate_grads, up_grads = to_owners(gate_parts), to_owners(up_parts)

    head_back = dot_f32(mix_back, w_out, ((1,), (1,))).astype(BF16)
    out_part = held(dot_f32(mixed, mix_back, ((0,), (0,))), up_grads).astype(BF16)
    out_total = lax.psum(out_part, "expert")
    down_parts = expert_grad(act, rows_cot, n_shard, [out_total])
    down_grads = to_owners(down_parts)
    backs, head_gains, count = [], 0.0, heads // ATTENTION_PARTS
    for part in range(ATTENTION_PARTS):
        *back, gains = attention_back(
            qkv_pre, head_back, tables, heads, size, part * count, count
        )
        backs.append(back)
        head_gains = head_gains + gains
    qkv_back = jnp.concatenate([back[i] for i in range(3) for back in backs], axis=1)
    qkv_part = dot_f32(normed, qkv_back, ((0,), (0,))).astype(BF16)
    qkv_terms = qkv_part.reshape(n_shard, n_expert, slice_rows, 3 * local_width)
    qkv_mine, qkv_hops = ring_scatter(
        lambda r: lax.dynamic_index_in_dim(qkv_terms, source[r], 1, keepdims=False).reshape(
            n_shard * slice_rows, 3 * local_width
        ),
        n_expert,
        after=[gate_grads],
    )
    normed_back = dot_f32(held(qkv_back, qkv_hops[2], out_total), w_local, ((1,), (1,)))
    gain_one_part = jnp.sum(normed_back * token_float * scale_one, axis=0)
    own_back = shard_scatter(
        list(normed_back.astype(BF16).reshape(n_shard, rows, width))
    )
    tokens_grad = hidden_back + norm_back(own_back, own_tokens, scale_one[:rows], gain_one)

    def placed_blocks(blocks):
        total = jnp.zeros((n_expert * blocks[0].shape[0], blocks[0].shape[1]), F32)
        for r in arrivals(n_expert):
            total = lax.dynamic_update_slice(
                total, blocks[r].astype(F32), (source[r] * blocks[r].shape[0], 0)
            )
        return total

    qkv_mine = lax.all_to_all(
        qkv_mine.astype(BF16), "shard", split_axis=0, concat_axis=0, tiled=True
    )
    qkv_mine = (
        qkv_mine.reshape(n_shard, slice_rows, 3, local_width)
        .transpose(1, 2, 0, 3)
        .reshape(slice_rows, 3 * width)
    )
    qkv_total = placed_blocks(ring_gather(qkv_mine, n_expert))

    small = jnp.concatenate(
        [
            gain_one_part.reshape(n_shard, -1),
            gain_two_part.reshape(n_shard, -1),
            head_gains[0].reshape(n_shard, -1),
            head_gains[1].reshape(n_shard, -1),
            router_grad.reshape(n_shard, -1),
        ],
        axis=1,
    )
    small = held(small, qkv_hops[1])
    small = lax.all_to_all(small, "shard", split_axis=0, concat_axis=0, tiled=True)
    small = tree_sum(jnp.sum(small, axis=0).reshape(1, -1), "expert")[0]
    gate_up_grad = jnp.stack([gate_grads, up_grads], axis=1).astype(F32)
    return (
        layer_out,
        tokens_grad,
        small[: cuts[0]],
        qkv_total,
        small[cuts[1] : cuts[2]],
        small[cuts[2] : cuts[3]],
        out_total.astype(F32),
        small[cuts[0] : cuts[1]],
        small[cuts[3] :].reshape(part_rows, expert_count),
        gate_up_grad,
        down_grads.astype(F32),
    )


def solution(mesh):
    placed = (
        P(("expert", "shard"), None),
        P(("expert", "shard"), None),
        P(("expert", "shard"), None),
        P("expert"),
        P(),
        P("shard"),
        P("shard", None),
        P("shard"),
        P("shard"),
        P("shard", None),
        P("shard"),
        P("shard", None),
        P("expert", None, None, "shard"),
        P("expert", "shard", None),
    )
    return jax.shard_map(
        on_device,
        mesh=mesh,
        in_specs=placed,
        out_specs=(
            P(("expert", "shard"), None),
            P(("expert", "shard"), None),
            P("shard"),
            P("shard", None),
            P("shard"),
            P("shard"),
            P("shard", None),
            P("shard"),
            P("shard", None),
            P("expert", None, None, "shard"),
            P("expert", "shard", None),
        ),
        check_vma=False,
    )
```

```python
import functools

import jax
import jax.numpy as jnp
from jax import lax
from jax.experimental import pallas as pl
from jax.experimental.pallas import tpu as pltpu
from jax.sharding import PartitionSpec as P

HEADS = 16
EPS = 1e-06
THETA = 50000.0
NEG_BIG = -1e30
F32 = jnp.float32
BF16 = jnp.bfloat16


def dot_f32(left, right, dims):
    return lax.dot_general(left, right, (dims, ((), ())), preferred_element_type=F32)


def rms_scale(values):
    return lax.rsqrt(jnp.mean(values * values, axis=-1, keepdims=True) + EPS)


def norm_back(grad_in, values, scale, gain):
    weighted = grad_in * gain
    return scale * weighted - values * scale**3 * jnp.mean(
        weighted * values, axis=-1, keepdims=True
    )


def ring_order(size):
    if size == 8:
        return [0, 2, 4, 6, 7, 5, 3, 1]
    return list(range(size))


def ring_perms(size):
    order = ring_order(size)
    ahead = [(order[i], order[(i + 1) % size]) for i in range(size)]
    return ahead, [(b, a) for a, b in ahead]


def ring_place(size):
    order = ring_order(size)
    places = [0] * size
    for place, index in enumerate(order):
        places[index] = place
    mine = jnp.array(places, jnp.int32)[lax.axis_index("expert")]
    source = jnp.array(order, jnp.int32)[
        jnp.mod(mine - jnp.arange(size, dtype=jnp.int32), size)
    ]
    behind = jnp.mod(mine - jnp.array(places, jnp.int32), size)
    return source, behind


def tied(value, *others):
    return lax.optimization_barrier((value, others))[0]


def zero_of(*others):
    total = jnp.zeros((), F32)
    for other in jax.tree.leaves(others):
        total = total + jnp.minimum(jnp.abs(other[(0,) * other.ndim].astype(F32)), 0.0)
    return total


def held(value, *others):
    return value + zero_of(*others).astype(value.dtype)


def ring_gather(block, size, whole=True):
    ahead, back = ring_perms(size)
    first = (lax.ppermute(block, "expert", ahead), lax.ppermute(block, "expert", back))
    return ring_rest(block, first, size, {}, whole)


def ring_rest(block, first, size, gates, whole=True):
    ahead, back = ring_perms(size)
    blocks = [block] * size
    from_behind, from_ahead = first
    blocks[1], blocks[size - 1] = first
    for step in range(2, size // 2):
        if step in gates:
            from_behind, from_ahead = tied((from_behind, from_ahead), gates[step])
        from_behind = lax.ppermute(from_behind, "expert", ahead)
        from_ahead = lax.ppermute(from_ahead, "expert", back)
        blocks[step] = from_behind
        blocks[size - step] = from_ahead
    if whole:
        ring_last(blocks, size)
    return blocks


def ring_last(blocks, size, after=()):
    ahead, back = ring_perms(size)
    half = blocks[0].shape[0] // 2
    top, bottom = blocks[size // 2 - 1][:half], blocks[size // 2 + 1][half:]
    if after:
        top, bottom = held(top, after), held(bottom, after)
    blocks[size // 2] = jnp.concatenate(
        [lax.ppermute(top, "expert", ahead), lax.ppermute(bottom, "expert", back)], axis=0
    )


def arrivals(size):
    order = [0]
    for step in range(1, size // 2):
        order += [step, size - step]
    return order + [size // 2]


def ring_scatter(pick, size, after=(), brought=None):
    ahead, back = ring_perms(size)
    first = pick(size // 2)
    if after:
        first = held(first, after)
    half = first.shape[0] // 2
    down = lax.ppermute(first[:half].astype(BF16), "expert", back)
    up = lax.ppermute(first[half:].astype(BF16), "expert", ahead)
    hops = [] if brought is None else brought
    hops.append(down)
    for step in range(size // 2 - 1, 0, -1):
        own_down, own_up = pick(step).astype(F32), pick(size - step).astype(F32)
        if step == size // 2 - 1:
            zeros = jnp.zeros_like(down)
            down = jnp.concatenate([down, zeros], axis=0)
            up = jnp.concatenate([zeros, up], axis=0)
        both = zero_of(down, up)
        down, up = (
            lax.ppermute((own_down + down.astype(F32) + both).astype(BF16), "expert", back),
            lax.ppermute((own_up + up.astype(F32) + both).astype(BF16), "expert", ahead),
        )
        hops.append(down)
    return pick(0).astype(F32) + down.astype(F32) + up.astype(F32), hops


def swap(value, bit):
    size = lax.axis_size("shard")
    return lax.ppermute(value, "shard", [(i, i ^ bit) for i in range(size)])


def shard_gather(block):
    far = swap(block, 2)
    near = swap(block, 1)
    return [block, near, far, swap(far, 1)]


def shard_scatter(blocks):
    near = [swap(blocks[3].astype(BF16), 1), swap(blocks[1].astype(BF16), 1)]
    far = swap((blocks[2].astype(F32) + near[0].astype(F32)).astype(BF16), 2)
    return blocks[0].astype(F32) + near[1].astype(F32) + far.astype(F32)


def tree_sum(value, axis):
    size = lax.axis_size(axis)
    bit = 1
    while bit < size:
        value = value + lax.ppermute(value, axis, [(i, i ^ bit) for i in range(size)])
        bit *= 2
    return value


def turned(values, cosines, sines):
    return values * cosines + pltpu.roll(values, values.shape[-1] // 2, 1) * sines


def attention_kernel(scale, chunk, q_ref, k_ref, v_ref, cos_ref, sin_ref, col_ref, row_ref, gq_ref, gk_ref, out_ref):
    cosines, sines = cos_ref[...], sin_ref[...]
    q_pre, k_pre = q_ref[...], k_ref[...]
    query = turned(q_pre * rms_scale(q_pre) * gq_ref[...], cosines, sines).astype(BF16)
    key = turned(k_pre * rms_scale(k_pre) * gk_ref[...], cosines, sines).astype(BF16)
    value = v_ref[...].astype(BF16)
    docs = row_ref[...]
    for start in range(0, q_pre.shape[0], chunk):
        rows = slice(start, start + chunk)
        scores = dot_f32(query[rows], key, ((1,), (1,))) * scale
        scores = jnp.where(col_ref[rows, :] == docs, scores, NEG_BIG)
        shifted = jnp.exp(scores - jnp.max(scores, axis=-1, keepdims=True))
        probs = shifted * (1.0 / jnp.sum(shifted, axis=-1, keepdims=True))
        out_ref[rows, :] = dot_f32(probs.astype(BF16), value, ((1,), (0,))).astype(BF16)


def attention_back_kernel(
    scale, chunk, q_ref, k_ref, v_ref, do_ref, cos_ref, sin_ref, col_ref, row_ref, gq_ref, gk_ref,
    dq_ref, dk_ref, dv_ref, gains_ref, dq_acc, dk_acc, dv_acc,
):
    cosines, sines = cos_ref[...], sin_ref[...]
    q_pre, k_pre = q_ref[...], k_ref[...]
    q_scale, k_scale = rms_scale(q_pre), rms_scale(k_pre)
    query = turned(q_pre * q_scale * gq_ref[...], cosines, sines).astype(BF16)
    key = turned(k_pre * k_scale * gk_ref[...], cosines, sines).astype(BF16)
    value = v_ref[...].astype(BF16)
    docs = row_ref[...]
    for start in range(0, q_pre.shape[0], chunk):
        rows = slice(start, start + chunk)
        out_back = do_ref[rows, :]
        scores = dot_f32(query[rows], key, ((1,), (1,))) * scale
        scores = jnp.where(col_ref[rows, :] == docs, scores, NEG_BIG)
        shifted = jnp.exp(scores - jnp.max(scores, axis=-1, keepdims=True))
        probs = shifted * (1.0 / jnp.sum(shifted, axis=-1, keepdims=True))
        prob_back = dot_f32(out_back, value, ((1,), (1,)))
        score_back = (
            probs * (prob_back - jnp.sum(probs * prob_back, axis=-1, keepdims=True))
        ).astype(BF16)
        dq_acc[rows, :] = dot_f32(score_back, key, ((1,), (0,)))
        dk_part = dot_f32(score_back, query[rows], ((0,), (0,)))
        dv_part = dot_f32(probs.astype(BF16), out_back, ((0,), (0,)))
        if start == 0:
            dk_acc[...] = dk_part
            dv_acc[...] = dv_part
        else:
            dk_acc[...] += dk_part
            dv_acc[...] += dv_part
    dv_ref[...] = dv_acc[...].astype(BF16)

    @pl.when(pl.program_id(0) == 0)
    def _():
        gains_ref[...] = jnp.zeros_like(gains_ref)

    for place, (acc, pre, pre_scale, gain, out) in enumerate(
        (
            (dq_acc, q_pre, q_scale, gq_ref[...], dq_ref),
            (dk_acc, k_pre, k_scale, gk_ref[...], dk_ref),
        )
    ):
        grad = turned((acc[...] * scale).astype(BF16).astype(F32), cosines, -sines)
        gains_ref[place : place + 1, :] += jnp.sum(grad * pre * pre_scale, axis=0, keepdims=True)
        out[...] = norm_back(grad, pre, pre_scale, gain).astype(BF16)


def attention_specs(length, size, heads, first=0):
    def column(part):
        return pl.BlockSpec((length, size), lambda h: (0, part * heads + first + h))

    def whole(*shape):
        return pl.BlockSpec(shape, lambda h: (0, 0))

    pre = [column(0), column(1), column(2)]
    rest = [
        whole(length, size),
        whole(length, size),
        whole(length, 1),
        whole(1, length),
        whole(1, size),
        whole(1, size),
    ]
    return column(0), pre, rest


def attention(qkv_pre, tables, heads, size):
    length = qkv_pre.shape[0]
    own, pre, rest = attention_specs(length, size, heads)
    return pl.pallas_call(
        functools.partial(attention_kernel, size**-0.5, min(256, length)),
        grid=(heads,),
        in_specs=pre + rest,
        out_specs=own,
        out_shape=jax.ShapeDtypeStruct((length, heads * size), BF16),
        cost_estimate=pl.CostEstimate(
            flops=4 * heads * length * length * size,
            bytes_accessed=qkv_pre.size * 4 + length * heads * size * 2,
            transcendentals=heads * length * length,
        ),
        name="attention",
    )(qkv_pre, qkv_pre, qkv_pre, *tables)


def attention_back(qkv_pre, head_back, tables, heads, size, first, count):
    length = qkv_pre.shape[0]
    given, pre, rest = attention_specs(length, size, heads, first)
    own = pl.BlockSpec((length, size), lambda h: (0, h))
    shape = jax.ShapeDtypeStruct((length, count * size), BF16)
    return pl.pallas_call(
        functools.partial(attention_back_kernel, size**-0.5, min(256, length)),
        grid=(count,),
        in_specs=pre + [given] + rest,
        out_specs=[own, own, own, pl.BlockSpec((2, size), lambda h: (0, 0))],
        out_shape=[shape, shape, shape, jax.ShapeDtypeStruct((2, size), F32)],
        scratch_shapes=[pltpu.VMEM((length, size), F32)] * 3,
        cost_estimate=pl.CostEstimate(
            flops=10 * count * length * length * size,
            bytes_accessed=qkv_pre.size * 4 + 4 * length * count * size * 2,
            transcendentals=heads * length * length,
        ),
        name="attention_back",
    )(qkv_pre, qkv_pre, qkv_pre, head_back, *tables)


GROUP = 4
ATTENTION_PARTS = 1


def block_groups(size):
    if size == 8:
        return [[0, 1, 7], [2, 6], [4, 3, 5]]
    order = arrivals(size)
    return [order[i : i + GROUP] for i in range(0, size, GROUP)]


VMEM_BYTES = 60 * 1024 * 1024


def expert_kernel(count, extras, base_ref, *refs):
    refs = refs[extras:]
    x_refs, dy_refs = refs[:count], refs[count : 2 * count]
    slot_ref, router_ref, wg_ref, wu_ref, wd_ref = refs[2 * count : 2 * count + 5]
    rin_ref, rcot_ref, act_ref, gb_ref, ub_ref, rback_ref = refs[
        2 * count + 5 : 2 * count + 11
    ]
    weight_ref, gg_ref = refs[2 * count + 11 :]
    expert, part = pl.program_id(0), pl.program_id(1)
    tokens = x_refs[0].shape[0]
    slots = rin_ref.shape[1] // count

    def pick_of(block):
        places = lax.broadcasted_iota(jnp.int32, (slots, tokens), 0)
        return places == slot_ref[0, block : block + 1, :]

    def low(mask):
        return jnp.where(mask, 1.0, 0.0).astype(BF16)

    @pl.when(part == 0)
    def _():
        mine = base_ref[0] + expert
        for block in range(count):
            rows = pl.ds(block * slots, slots)
            pick = pick_of(block)
            pick_low = low(pick)
            x_block = x_refs[block][...]
            rin_ref[0, rows, :] = dot_f32(pick_low, x_block, ((1,), (0,))).astype(BF16)
            rcot_ref[0, rows, :] = dot_f32(
                pick_low, dy_refs[block][...], ((1,), (0,))
            ).astype(BF16)
            logits = dot_f32(router_ref[...], x_block, ((1,), (1,)))
            powers = jnp.exp(logits - jnp.max(logits, axis=0, keepdims=True))
            router = powers / jnp.sum(powers, axis=0, keepdims=True)
            which = lax.broadcasted_iota(jnp.int32, router.shape, 0)
            gate = jnp.sum(jnp.where(which == mine, router, 0.0), axis=0, keepdims=True)
            weight_ref[rows, :] = jnp.sum(
                jnp.where(pick, gate, 0.0), axis=1, keepdims=True
            )

    rows_in, rows_cot = rin_ref[0], rcot_ref[0]
    w_gate, w_up, w_back = wg_ref[0, 0, 0], wu_ref[0, 0, 0], wd_ref[0, 0]
    weight = weight_ref[...]
    pre_gate = dot_f32(rows_in, w_gate, ((1,), (0,)))
    pre_up = dot_f32(rows_in, w_up, ((1,), (0,)))
    cot_down = dot_f32(rows_cot, w_back, ((1,), (1,)))
    sigmoid = jax.nn.sigmoid(pre_gate)
    silu = pre_gate * sigmoid
    act = silu * pre_up
    share = act * cot_down
    folded = share[:, :128]
    for lane in range(128, share.shape[1], 128):
        folded = folded + share[:, lane : lane + 128]
    act_back = weight * cot_down
    act_ref[0] = (weight * act).astype(BF16)
    gb_ref[0] = (act_back * pre_up * (sigmoid + silu * (1.0 - sigmoid))).astype(BF16)
    ub_ref[0] = (act_back * silu).astype(BF16)

    @pl.when(part == 0)
    def _():
        gg_ref[...] = folded

    @pl.when(part > 0)
    def _():
        gg_ref[...] += folded

    @pl.when(part == pl.num_programs(1) - 1)
    def _():
        for block in range(count):
            rows = pl.ds(block * slots, slots)
            pick = pick_of(block)
            share = jnp.sum(gg_ref[rows, :], axis=1, keepdims=True)
            rback_ref[0, block : block + 1, :] = jnp.sum(
                jnp.where(pick, share, 0.0), axis=0, keepdims=True
            )


def weight_spec(shape, which=None):
    if which is None:
        return pl.BlockSpec((1, 1) + shape[2:], lambda e, j: (j, e, 0, 0))
    return pl.BlockSpec((1, 1, 1) + shape[3:], lambda e, j: (j, e, which, 0, 0))


def expert_group(base, x_blocks, dy_blocks, slot_of, router_rows, w_gate_up, w_down, slots, after):
    count = len(x_blocks)
    tokens, width = x_blocks[0].shape
    parts, experts, hidden = w_down.shape[:3]
    rows = count * slots

    def still(shape):
        return pl.BlockSpec(
            shape, lambda e, j: (0,) * len(shape), pipeline_mode=pl.Buffered(1)
        )

    def per_expert(*shape):
        return pl.BlockSpec((1,) + shape, lambda e, j: (e, 0, 0))

    part = pl.BlockSpec((1, rows, hidden), lambda e, j: (e, 0, j))
    wide = jax.ShapeDtypeStruct((experts, rows, width), BF16)
    deep = jax.ShapeDtypeStruct((experts, rows, parts * hidden), BF16)
    flops = 6 * rows * width * parts * hidden * experts
    return pl.pallas_call(
        functools.partial(expert_kernel, count, len(after)),
        grid=(experts, parts),
        in_specs=[pl.BlockSpec(memory_space=pltpu.SMEM)]
        + [pl.BlockSpec(memory_space=pl.ANY)] * len(after)
        + [still((tokens, width))] * (2 * count)
        + [
            per_expert(count, tokens),
            still(router_rows.shape),
            weight_spec(w_gate_up.shape, 0),
            weight_spec(w_gate_up.shape, 1),
            weight_spec(w_down.shape),
        ],
        out_specs=[
            per_expert(rows, width),
            per_expert(rows, width),
            part,
            part,
            part,
            per_expert(count, tokens),
        ],
        out_shape=[
            wide,
            wide,
            deep,
            deep,
            deep,
            jax.ShapeDtypeStruct((experts, count, tokens), F32),
        ],
        scratch_shapes=[
            pltpu.VMEM((rows, 1), F32),
            pltpu.VMEM((rows, 128), F32),
        ],
        compiler_params=pltpu.CompilerParams(vmem_limit_bytes=VMEM_BYTES),
        cost_estimate=pl.CostEstimate(
            flops=flops, bytes_accessed=3 * w_gate_up.size, transcendentals=rows * parts * hidden
        ),
        name="experts",
    )(base, *after, *x_blocks, *dy_blocks, slot_of, router_rows, w_gate_up, w_gate_up, w_down)


def combine_kernel(count, pairs, dim, slot_ref, *refs):
    lefts, weights = refs[:pairs], refs[pairs : 2 * pairs]
    terms_ref, acc_ref, sum_ref = refs[-3:]
    expert, part = pl.program_id(0), pl.program_id(1)
    tokens = terms_ref.shape[1]
    slots = acc_ref.shape[0] // count
    out = None
    for left, weight in zip(lefts, weights):
        matrix = weight[(0,) * (len(weight.shape) - 2)]
        product = dot_f32(left[0], matrix, ((1,), (dim,)))
        out = product if out is None else out + product

    @pl.when(part == 0)
    def _():
        acc_ref[...] = out

    @pl.when(part > 0)
    def _():
        acc_ref[...] += out

    @pl.when(part == pl.num_programs(1) - 1)
    def _():
        for block in range(count):
            places = lax.broadcasted_iota(jnp.int32, (slots, tokens), 0)
            pick = jnp.where(places == slot_ref[0, block : block + 1, :], 1.0, 0.0).astype(BF16)
            rows = acc_ref[pl.ds(block * slots, slots), :].astype(BF16)
            term = dot_f32(pick, rows, ((0,), (0,)))

            @pl.when(expert == 0)
            def _():
                sum_ref[block] = term

            @pl.when(expert > 0)
            def _():
                sum_ref[block] += term

            @pl.when(expert == pl.num_programs(0) - 1)
            def _():
                terms_ref[block] = sum_ref[block].astype(BF16)


def expert_combine(slot_of, lefts, weight, dim, after):
    experts, count, tokens = slot_of.shape
    parts = weight.shape[0]
    hidden, width = weight.shape[-2:] if dim == 0 else weight.shape[-1:-3:-1]
    rows = lefts[0].shape[1]
    pairs = len(lefts)
    which = range(pairs) if pairs > 1 else [None]
    return pl.pallas_call(
        functools.partial(combine_kernel, count, pairs, dim),
        grid=(experts, parts),
        in_specs=[pl.BlockSpec((1, count, tokens), lambda e, j: (e, 0, 0))]
        + [pl.BlockSpec((1, rows, hidden), lambda e, j: (e, 0, j))] * pairs
        + [weight_spec(weight.shape, place) for place in which]
        + [pl.BlockSpec(memory_space=pl.ANY)] * len(after),
        out_specs=pl.BlockSpec((count, tokens, width), lambda e, j: (0, 0, 0)),
        out_shape=jax.ShapeDtypeStruct((count, tokens, width), BF16),
        scratch_shapes=[
            pltpu.VMEM((rows, width), F32),
            pltpu.VMEM((count, tokens, width), F32),
        ],
        compiler_params=pltpu.CompilerParams(vmem_limit_bytes=VMEM_BYTES),
        cost_estimate=pl.CostEstimate(
            flops=2 * pairs * rows * width * parts * hidden * experts,
            bytes_accessed=2 * (weight.size + pairs * lefts[0].size + count * tokens * width),
            transcendentals=0,
        ),
        name="expert_combine",
    )(slot_of, *lefts, *[weight] * pairs, *after)


def grad_kernel(groups, *refs):
    total = None
    for left, right in zip(refs[:groups], refs[groups : 2 * groups]):
        part = dot_f32(left[0], right[0], ((0,), (0,)))
        total = part if total is None else total + part
    refs[-1][0, 0] = total.astype(BF16)


def expert_grad(lefts, rights, parts, after):
    experts = lefts[0].shape[0]
    hidden = min(lefts[0].shape[2], rights[0].shape[2]) // parts

    def spec(array, cut):
        width = hidden if cut else array.shape[2]
        return pl.BlockSpec(
            (1, array.shape[1], width), lambda e, j: (e, 0, j if cut else 0)
        )

    cut_left = lefts[0].shape[2] < rights[0].shape[2]
    shape = (
        hidden if cut_left else lefts[0].shape[2],
        rights[0].shape[2] if cut_left else hidden,
    )
    rows = sum(left.shape[1] for left in lefts)
    return pl.pallas_call(
        functools.partial(grad_kernel, len(lefts)),
        grid=(experts, parts),
        in_specs=[spec(left, cut_left) for left in lefts]
        + [spec(right, not cut_left) for right in rights]
        + [pl.BlockSpec(memory_space=pl.ANY)] * len(after),
        out_specs=pl.BlockSpec((1, 1) + shape, lambda e, j: (j, e, 0, 0)),
        out_shape=jax.ShapeDtypeStruct((parts, experts) + shape, BF16),
        compiler_params=pltpu.CompilerParams(vmem_limit_bytes=VMEM_BYTES),
        cost_estimate=pl.CostEstimate(
            flops=2 * rows * shape[0] * shape[1] * parts * experts,
            bytes_accessed=2 * experts * (parts * shape[0] * shape[1] + 3 * rows * shape[0]),
            transcendentals=0,
        ),
        name="expert_grad",
    )(*lefts, *rights, *after)


def on_device(
    tokens,
    out_grad,
    routes,
    segments,
    capacity,
    attn_gain,
    w_qkv,
    query_gain,
    key_gain,
    w_out,
    ffn_gain,
    w_router,
    w_gate_up,
    w_down,
):
    n_expert = lax.axis_size("expert")
    n_shard = lax.axis_size("shard")
    rows, width = tokens.shape
    size = width // HEADS
    heads = HEADS // n_shard
    local_width = heads * size
    length = segments.shape[0]
    expert_count = capacity.shape[0]
    local_experts = w_down.shape[0]
    slots = rows * routes.shape[1] // expert_count
    shard_index = lax.axis_index("shard")
    expert_index = lax.axis_index("expert")
    source, behind = ring_place(n_expert)
    part_rows = w_qkv.shape[0]
    slice_rows = part_rows // n_expert
    relative = jnp.bitwise_xor(shard_index, jnp.arange(n_shard, dtype=jnp.int32))

    packed = jnp.concatenate(
        [attn_gain, ffn_gain, query_gain, key_gain, w_router.reshape(-1)]
    )
    packed = lax.all_to_all(
        jnp.broadcast_to(packed[None], (n_shard, packed.shape[0])), "shard", 0, 0, tiled=True
    )
    cuts = [part_rows, 2 * part_rows, 2 * part_rows + size // n_shard]
    cuts.append(cuts[-1] + size // n_shard)
    gain_one = packed[:, : cuts[0]].reshape(1, width).astype(F32)
    gain_two = packed[:, cuts[0] : cuts[1]].reshape(1, width).astype(F32)
    gain_query = packed[:, cuts[1] : cuts[2]].reshape(1, size).astype(F32)
    gain_key = packed[:, cuts[2] : cuts[3]].reshape(1, size).astype(F32)
    full_router = packed[:, cuts[3] :].reshape(width, expert_count)
    router_rows = full_router.T

    own_slice = lax.dynamic_slice_in_dim(w_qkv, expert_index * slice_rows, slice_rows)
    own_slice = own_slice.reshape(slice_rows, 3, n_shard, local_width).transpose(2, 0, 1, 3)
    own_slice = lax.all_to_all(
        own_slice.reshape(n_shard, slice_rows, 3 * local_width), "shard", 0, 0, tiled=True
    )
    own_slice = own_slice.reshape(n_shard * slice_rows, 3 * local_width)

    ahead, back = ring_perms(n_expert)
    dy_first = (
        lax.ppermute(out_grad, "expert", ahead),
        lax.ppermute(out_grad, "expert", back),
    )
    w_blocks = ring_gather(tied(own_slice, dy_first), n_expert)
    w_local = jnp.zeros((n_shard, n_expert, slice_rows, 3 * local_width), BF16)
    for r in arrivals(n_expert):
        w_local = lax.dynamic_update_slice(
            w_local,
            w_blocks[r].reshape(n_shard, 1, slice_rows, 3 * local_width),
            (0, source[r], 0, 0),
        )
    w_local = w_local.reshape(width, 3 * local_width)

    token_parts = shard_gather(tied(tokens, own_slice))
    token_blocks = jnp.concatenate(token_parts, axis=0)

    routes_all = lax.all_to_all(
        jnp.broadcast_to(routes[None], (n_expert,) + routes.shape), "expert", 0, 0, tiled=True
    )[source]

    gate_up_full = lax.all_gather(w_gate_up, "shard")
    down_full = lax.all_gather(w_down, "shard")

    my_experts = expert_index * local_experts + jnp.arange(local_experts, dtype=jnp.int32)
    named = jnp.any(
        routes_all[None, :, :, :] == my_experts[:, None, None, None], axis=3
    )
    order = jnp.arange(rows, dtype=jnp.int32)
    before = (order[:, None] < order[None, :]).astype(BF16)
    earlier = jnp.einsum(
        "ebu,ut->ebt", named.astype(BF16), before, preferred_element_type=F32
    ).astype(jnp.int32)
    my_limits = lax.dynamic_slice_in_dim(capacity, expert_index * local_experts, local_experts)
    slot_of = jnp.where(named & (earlier < my_limits[:, None, None]), earlier, -1)

    position = (
        relative[:, None] * rows + jnp.arange(rows, dtype=jnp.int32)[None, :]
    ).reshape(-1).astype(F32)
    half_size = size // 2
    frequency = THETA ** (-(2.0 * jnp.arange(half_size, dtype=F32)) / size)
    angles = position[:, None] * frequency[None, :]
    cosines, sines = jnp.cos(angles), jnp.sin(angles)
    docs = segments.reshape(n_shard, rows)[relative].reshape(-1)
    tables = (
        jnp.concatenate([cosines, cosines], axis=1),
        jnp.concatenate([-sines, sines], axis=1),
        docs[:, None],
        docs[None, :],
        gain_query,
        gain_key,
    )

    token_float = token_blocks.astype(F32)
    scale_one = rms_scale(token_float)
    normed = (token_float * scale_one * gain_one).astype(BF16)
    qkv_pre = jnp.dot(normed, w_local, preferred_element_type=F32)
    mixed = attention(qkv_pre, tables, heads, size)
    dy_blocks = ring_rest(
        out_grad, dy_first, n_expert, {2: w_blocks[n_expert // 2], 3: mixed}
    )
    attended = jnp.dot(tied(mixed, dy_blocks[2]), w_out, preferred_element_type=F32).astype(BF16)
    own_tokens = tokens.astype(F32)
    hidden = own_tokens + shard_scatter(list(attended.reshape(n_shard, rows, width)))
    scale_two = rms_scale(hidden)
    ffn_low = (
        hidden * scale_two * gain_two
        + zero_of(dy_blocks[n_expert // 2 - 1], dy_blocks[n_expert // 2 + 1])
    ).astype(BF16)
    router = jax.nn.softmax(
        jnp.dot(ffn_low, full_router, preferred_element_type=F32), axis=-1
    )

    ffn_blocks = ring_gather(tied(ffn_low, dy_blocks[3]), n_expert, whole=False)
    groups = block_groups(n_expert)
    base = (expert_index * local_experts).reshape(1).astype(jnp.int32)
    results, slot_groups = [], []
    for group in groups:
        slots_g = jnp.stack([slot_of[:, r] for r in group], axis=1)
        if n_expert // 2 in group:
            ring_last(ffn_blocks, n_expert, [results[0][-1]] if results else ())
        slot_groups.append(slots_g)
        results.append(
            expert_group(
                base,
                [ffn_blocks[r] for r in group],
                [dy_blocks[r] for r in group],
                slot_groups[-1],
                router_rows,
                gate_up_full,
                down_full,
                slots,
                [results[-1][-1]] if results else [],
            )
        )
    rows_in, rows_cot, act, gate_back, up_back, router_terms = map(list, zip(*results))
    where_is = {r: (g, i) for g, group in enumerate(groups) for i, r in enumerate(group)}

    def picker(arrays):
        return lambda r: arrays[where_is[r][0]][where_is[r][1]]

    out_terms, terms = [None] * len(groups), [None] * len(groups)
    latest = router_terms[-1]
    last = len(groups) - 1
    out_hops = []

    def pick_out(r):
        g, place_in = where_is[r]
        if out_terms[g] is None:
            after = [out_terms[g + 1]] if g < last else [router_terms[-1]]
            after += out_hops[:1] if g == 0 else []
            out_terms[g] = expert_combine(slot_groups[g], [act[g]], down_full, 0, after)
        return out_terms[g][place_in]

    for g in range(last, 0, -1):
        pick_out(groups[g][0])
    out_sum, _ = ring_scatter(pick_out, n_expert, brought=out_hops)
    layer_out = (hidden + out_sum).astype(BF16)
    latest = out_terms[0]
    for g in range(last, -1, -1):
        latest = terms[g] = expert_combine(
            slot_groups[g],
            [gate_back[g], up_back[g]],
            gate_up_full,
            1,
            [latest] + (out_hops[1:2] if g == last - 1 else []),
        )
    back_hops = []
    ffn_back, _ = ring_scatter(picker(terms), n_expert, after=out_hops[2:3], brought=back_hops)
    back_to = jnp.stack(
        [router_terms[where_is[r][0]][:, where_is[r][1]] for r in range(n_expert)]
    )
    router_back = lax.all_to_all(
        back_to[behind], "expert", split_axis=0, concat_axis=0, tiled=True
    ).reshape(expert_count, rows).T

    gate_parts = expert_grad(rows_in, gate_back, n_shard, [latest] + out_hops[2:3])
    up_parts = expert_grad(rows_in, up_back, n_shard, [gate_parts] + back_hops[:1])
    down_parts = expert_grad(act, rows_cot, n_shard, [up_parts] + back_hops[1:2])
    ffn_back = ffn_back + zero_of(down_parts)

    logit_back = (
        router * (router_back - jnp.sum(router * router_back, axis=-1, keepdims=True))
    ).astype(BF16)
    router_grad = dot_f32(ffn_low, logit_back, ((0,), (0,)))
    ffn_back = ffn_back + dot_f32(logit_back, full_router, ((1,), (1,)))
    gain_two_part = jnp.sum(ffn_back * hidden * scale_two, axis=0)
    hidden_back = out_grad.astype(F32) + norm_back(ffn_back, hidden, scale_two, gain_two)

    hidden_low = hidden_back.astype(BF16)
    mix_parts = shard_gather(hidden_low)
    mix_back = jnp.concatenate(mix_parts, axis=0)

    gate_grads, up_grads, down_grads = (
        lax.psum_scatter(
            parts.reshape((n_shard * local_experts,) + parts.shape[2:]),
            "shard",
            scatter_dimension=0,
            tiled=True,
        ).astype(F32)
        for parts in (gate_parts, up_parts, down_parts)
    )

    head_back = dot_f32(mix_back, w_out, ((1,), (1,))).astype(BF16)
    out_part = dot_f32(mixed, mix_back, ((0,), (0,))).astype(BF16)
    backs, head_gains, count = [], 0.0, heads // ATTENTION_PARTS
    for part in range(ATTENTION_PARTS):
        *back, gains = attention_back(
            qkv_pre, head_back, tables, heads, size, part * count, count
        )
        backs.append(back)
        head_gains = head_gains + gains
    qkv_back = jnp.concatenate([back[i] for i in range(3) for back in backs], axis=1)
    qkv_part = dot_f32(normed, qkv_back, ((0,), (0,))).astype(BF16)
    qkv_terms = qkv_part.reshape(n_shard, n_expert, slice_rows, 3 * local_width)
    qkv_mine, qkv_hops = ring_scatter(
        lambda r: lax.dynamic_index_in_dim(qkv_terms, source[r], 1, keepdims=False).reshape(
            n_shard * slice_rows, 3 * local_width
        ),
        n_expert,
    )
    normed_back = dot_f32(held(qkv_back, qkv_hops[1]), w_local, ((1,), (1,)))
    gain_one_part = jnp.sum(normed_back * token_float * scale_one, axis=0)
    own_back = shard_scatter(
        list(normed_back.astype(BF16).reshape(n_shard, rows, width))
    )
    tokens_grad = hidden_back + norm_back(own_back, own_tokens, scale_one[:rows], gain_one)

    def placed_blocks(blocks):
        total = jnp.zeros((n_expert * blocks[0].shape[0], blocks[0].shape[1]), F32)
        for r in arrivals(n_expert):
            total = lax.dynamic_update_slice(
                total, blocks[r].astype(F32), (source[r] * blocks[r].shape[0], 0)
            )
        return total

    out_total = lax.psum(out_part, "expert").astype(F32)
    qkv_mine = lax.all_to_all(
        qkv_mine.astype(BF16), "shard", split_axis=0, concat_axis=0, tiled=True
    )
    qkv_mine = (
        qkv_mine.reshape(n_shard, slice_rows, 3, local_width)
        .transpose(1, 2, 0, 3)
        .reshape(slice_rows, 3 * width)
    )
    qkv_total = placed_blocks(ring_gather(qkv_mine, n_expert))

    small = jnp.concatenate(
        [
            gain_one_part.reshape(n_shard, -1),
            gain_two_part.reshape(n_shard, -1),
            head_gains[0].reshape(n_shard, -1),
            head_gains[1].reshape(n_shard, -1),
            router_grad.reshape(n_shard, -1),
        ],
        axis=1,
    )
    small = held(small, qkv_hops[1])
    small = lax.all_to_all(small, "shard", split_axis=0, concat_axis=0, tiled=True)
    small = tree_sum(jnp.sum(small, axis=0).reshape(1, -1), "expert")[0]
    gate_up_grad = jnp.stack([gate_grads, up_grads], axis=1)
    return (
        layer_out,
        tokens_grad,
        small[: cuts[0]],
        qkv_total,
        small[cuts[1] : cuts[2]],
        small[cuts[2] : cuts[3]],
        out_total,
        small[cuts[0] : cuts[1]],
        small[cuts[3] :].reshape(part_rows, expert_count),
        gate_up_grad,
        down_grads,
    )


def solution(mesh):
    placed = (
        P(("expert", "shard"), None),
        P(("expert", "shard"), None),
        P(("expert", "shard"), None),
        P("expert"),
        P(),
        P("shard"),
        P("shard", None),
        P("shard"),
        P("shard"),
        P("shard", None),
        P("shard"),
        P("shard", None),
        P("expert", None, None, "shard"),
        P("expert", "shard", None),
    )
    return jax.shard_map(
        on_device,
        mesh=mesh,
        in_specs=placed,
        out_specs=(
            P(("expert", "shard"), None),
            P(("expert", "shard"), None),
            P("shard"),
            P("shard", None),
            P("shard"),
            P("shard"),
            P("shard", None),
            P("shard"),
            P("shard", None),
            P("expert", None, None, "shard"),
            P("expert", "shard", None),
        ),
        check_vma=False,
    )
```

```python
import functools

import jax
import jax.numpy as jnp
from jax import lax
from jax.experimental import pallas as pl
from jax.experimental.pallas import tpu as pltpu
from jax.sharding import PartitionSpec as P

HEADS = 16
EPS = 1e-06
THETA = 50000.0
NEG_BIG = -1e30
F32 = jnp.float32
BF16 = jnp.bfloat16


def dot_f32(left, right, dims):
    return lax.dot_general(left, right, (dims, ((), ())), preferred_element_type=F32)


def rms_scale(values):
    return lax.rsqrt(jnp.mean(values * values, axis=-1, keepdims=True) + EPS)


def norm_back(grad_in, values, scale, gain):
    weighted = grad_in * gain
    return scale * weighted - values * scale**3 * jnp.mean(
        weighted * values, axis=-1, keepdims=True
    )


def ring_order(size):
    if size == 8:
        return [0, 2, 4, 6, 7, 5, 3, 1]
    return list(range(size))


def ring_perms(size):
    order = ring_order(size)
    ahead = [(order[i], order[(i + 1) % size]) for i in range(size)]
    return ahead, [(b, a) for a, b in ahead]


def ring_place(size):
    order = ring_order(size)
    places = [0] * size
    for place, index in enumerate(order):
        places[index] = place
    mine = jnp.array(places, jnp.int32)[lax.axis_index("expert")]
    source = jnp.array(order, jnp.int32)[
        jnp.mod(mine - jnp.arange(size, dtype=jnp.int32), size)
    ]
    behind = jnp.mod(mine - jnp.array(places, jnp.int32), size)
    return source, behind


def tied(value, *others):
    return lax.optimization_barrier((value, others))[0]


def zero_of(*others):
    total = jnp.zeros((), F32)
    for other in jax.tree.leaves(others):
        total = total + jnp.minimum(jnp.abs(other[(0,) * other.ndim].astype(F32)), 0.0)
    return total


def held(value, *others):
    return value + zero_of(*others).astype(value.dtype)


def ring_gather(block, size, whole=True):
    ahead, back = ring_perms(size)
    first = (lax.ppermute(block, "expert", ahead), lax.ppermute(block, "expert", back))
    return ring_rest(block, first, size, {}, whole)


def ring_rest(block, first, size, gates, whole=True):
    ahead, back = ring_perms(size)
    blocks = [block] * size
    from_behind, from_ahead = first
    blocks[1], blocks[size - 1] = first
    for step in range(2, size // 2):
        if step in gates:
            from_behind, from_ahead = tied((from_behind, from_ahead), gates[step])
        from_behind = lax.ppermute(from_behind, "expert", ahead)
        from_ahead = lax.ppermute(from_ahead, "expert", back)
        blocks[step] = from_behind
        blocks[size - step] = from_ahead
    if whole:
        ring_last(blocks, size)
    return blocks


def ring_last(blocks, size, after=()):
    ahead, back = ring_perms(size)
    half = blocks[0].shape[0] // 2
    top, bottom = blocks[size // 2 - 1][:half], blocks[size // 2 + 1][half:]
    if after:
        top, bottom = held(top, after), held(bottom, after)
    blocks[size // 2] = jnp.concatenate(
        [lax.ppermute(top, "expert", ahead), lax.ppermute(bottom, "expert", back)], axis=0
    )


def arrivals(size):
    order = [0]
    for step in range(1, size // 2):
        order += [step, size - step]
    return order + [size // 2]


def ring_scatter(pick, size, after=(), brought=None):
    ahead, back = ring_perms(size)
    first = pick(size // 2)
    if after:
        first = held(first, after)
    half = first.shape[0] // 2
    down = lax.ppermute(first[:half].astype(BF16), "expert", back)
    up = lax.ppermute(first[half:].astype(BF16), "expert", ahead)
    hops = [] if brought is None else brought
    hops.append(down)
    for step in range(size // 2 - 1, 0, -1):
        own_down, own_up = pick(step).astype(F32), pick(size - step).astype(F32)
        if step == size // 2 - 1:
            zeros = jnp.zeros_like(down)
            down = jnp.concatenate([down, zeros], axis=0)
            up = jnp.concatenate([zeros, up], axis=0)
        both = zero_of(down, up)
        down, up = (
            lax.ppermute((own_down + down.astype(F32) + both).astype(BF16), "expert", back),
            lax.ppermute((own_up + up.astype(F32) + both).astype(BF16), "expert", ahead),
        )
        hops.append(down)
    return pick(0).astype(F32) + down.astype(F32) + up.astype(F32), hops


def swap(value, bit):
    size = lax.axis_size("shard")
    return lax.ppermute(value, "shard", [(i, i ^ bit) for i in range(size)])


def shard_gather(block):
    far = swap(block, 2)
    near = swap(block, 1)
    return [block, near, far, swap(far, 1)]


def shard_scatter(blocks):
    near = [swap(blocks[3].astype(BF16), 1), swap(blocks[1].astype(BF16), 1)]
    far = swap((blocks[2].astype(F32) + near[0].astype(F32)).astype(BF16), 2)
    return blocks[0].astype(F32) + near[1].astype(F32) + far.astype(F32)


def tree_sum(value, axis):
    size = lax.axis_size(axis)
    bit = 1
    while bit < size:
        value = value + lax.ppermute(value, axis, [(i, i ^ bit) for i in range(size)])
        bit *= 2
    return value


def turned(values, cosines, sines):
    return values * cosines + pltpu.roll(values, values.shape[-1] // 2, 1) * sines


def attention_kernel(scale, chunk, q_ref, k_ref, v_ref, cos_ref, sin_ref, col_ref, row_ref, gq_ref, gk_ref, out_ref):
    cosines, sines = cos_ref[...], sin_ref[...]
    q_pre, k_pre = q_ref[...], k_ref[...]
    query = turned(q_pre * rms_scale(q_pre) * gq_ref[...], cosines, sines).astype(BF16)
    key = turned(k_pre * rms_scale(k_pre) * gk_ref[...], cosines, sines).astype(BF16)
    value = v_ref[...].astype(BF16)
    docs = row_ref[...]
    for start in range(0, q_pre.shape[0], chunk):
        rows = slice(start, start + chunk)
        scores = dot_f32(query[rows], key, ((1,), (1,))) * scale
        scores = jnp.where(col_ref[rows, :] == docs, scores, NEG_BIG)
        shifted = jnp.exp(scores - jnp.max(scores, axis=-1, keepdims=True))
        probs = shifted * (1.0 / jnp.sum(shifted, axis=-1, keepdims=True))
        out_ref[rows, :] = dot_f32(probs.astype(BF16), value, ((1,), (0,))).astype(BF16)


def attention_back_kernel(
    scale, chunk, q_ref, k_ref, v_ref, do_ref, cos_ref, sin_ref, col_ref, row_ref, gq_ref, gk_ref,
    dq_ref, dk_ref, dv_ref, gains_ref, dq_acc, dk_acc, dv_acc,
):
    cosines, sines = cos_ref[...], sin_ref[...]
    q_pre, k_pre = q_ref[...], k_ref[...]
    q_scale, k_scale = rms_scale(q_pre), rms_scale(k_pre)
    query = turned(q_pre * q_scale * gq_ref[...], cosines, sines).astype(BF16)
    key = turned(k_pre * k_scale * gk_ref[...], cosines, sines).astype(BF16)
    value = v_ref[...].astype(BF16)
    docs = row_ref[...]
    for start in range(0, q_pre.shape[0], chunk):
        rows = slice(start, start + chunk)
        out_back = do_ref[rows, :]
        scores = dot_f32(query[rows], key, ((1,), (1,))) * scale
        scores = jnp.where(col_ref[rows, :] == docs, scores, NEG_BIG)
        shifted = jnp.exp(scores - jnp.max(scores, axis=-1, keepdims=True))
        probs = shifted * (1.0 / jnp.sum(shifted, axis=-1, keepdims=True))
        prob_back = dot_f32(out_back, value, ((1,), (1,)))
        score_back = (
            probs * (prob_back - jnp.sum(probs * prob_back, axis=-1, keepdims=True))
        ).astype(BF16)
        dq_acc[rows, :] = dot_f32(score_back, key, ((1,), (0,)))
        dk_part = dot_f32(score_back, query[rows], ((0,), (0,)))
        dv_part = dot_f32(probs.astype(BF16), out_back, ((0,), (0,)))
        if start == 0:
            dk_acc[...] = dk_part
            dv_acc[...] = dv_part
        else:
            dk_acc[...] += dk_part
            dv_acc[...] += dv_part
    dv_ref[...] = dv_acc[...].astype(BF16)

    @pl.when(pl.program_id(0) == 0)
    def _():
        gains_ref[...] = jnp.zeros_like(gains_ref)

    for place, (acc, pre, pre_scale, gain, out) in enumerate(
        (
            (dq_acc, q_pre, q_scale, gq_ref[...], dq_ref),
            (dk_acc, k_pre, k_scale, gk_ref[...], dk_ref),
        )
    ):
        grad = turned((acc[...] * scale).astype(BF16).astype(F32), cosines, -sines)
        gains_ref[place : place + 1, :] += jnp.sum(grad * pre * pre_scale, axis=0, keepdims=True)
        out[...] = norm_back(grad, pre, pre_scale, gain).astype(BF16)


def attention_specs(length, size, heads, first=0):
    def column(part):
        return pl.BlockSpec((length, size), lambda h: (0, part * heads + first + h))

    def whole(*shape):
        return pl.BlockSpec(shape, lambda h: (0, 0))

    pre = [column(0), column(1), column(2)]
    rest = [
        whole(length, size),
        whole(length, size),
        whole(length, 1),
        whole(1, length),
        whole(1, size),
        whole(1, size),
    ]
    return column(0), pre, rest


def attention(qkv_pre, tables, heads, size):
    length = qkv_pre.shape[0]
    own, pre, rest = attention_specs(length, size, heads)
    return pl.pallas_call(
        functools.partial(attention_kernel, size**-0.5, min(256, length)),
        grid=(heads,),
        in_specs=pre + rest,
        out_specs=own,
        out_shape=jax.ShapeDtypeStruct((length, heads * size), BF16),
        cost_estimate=pl.CostEstimate(
            flops=4 * heads * length * length * size,
            bytes_accessed=qkv_pre.size * 4 + length * heads * size * 2,
            transcendentals=heads * length * length,
        ),
        name="attention",
    )(qkv_pre, qkv_pre, qkv_pre, *tables)


def attention_back(qkv_pre, head_back, tables, heads, size, first, count):
    length = qkv_pre.shape[0]
    given, pre, rest = attention_specs(length, size, heads, first)
    own = pl.BlockSpec((length, size), lambda h: (0, h))
    shape = jax.ShapeDtypeStruct((length, count * size), BF16)
    return pl.pallas_call(
        functools.partial(attention_back_kernel, size**-0.5, min(256, length)),
        grid=(count,),
        in_specs=pre + [given] + rest,
        out_specs=[own, own, own, pl.BlockSpec((2, size), lambda h: (0, 0))],
        out_shape=[shape, shape, shape, jax.ShapeDtypeStruct((2, size), F32)],
        scratch_shapes=[pltpu.VMEM((length, size), F32)] * 3,
        cost_estimate=pl.CostEstimate(
            flops=10 * count * length * length * size,
            bytes_accessed=qkv_pre.size * 4 + 4 * length * count * size * 2,
            transcendentals=heads * length * length,
        ),
        name="attention_back",
    )(qkv_pre, qkv_pre, qkv_pre, head_back, *tables)


GROUP = 4
ATTENTION_PARTS = 1


def block_groups(size):
    if size == 8:
        return [[0, 1, 7], [2, 6], [4, 3, 5]]
    order = arrivals(size)
    return [order[i : i + GROUP] for i in range(0, size, GROUP)]


VMEM_BYTES = 60 * 1024 * 1024


def expert_kernel(count, extras, base_ref, *refs):
    refs = refs[extras:]
    x_refs, dy_refs = refs[:count], refs[count : 2 * count]
    slot_ref, router_ref, wg_ref, wu_ref, wd_ref = refs[2 * count : 2 * count + 5]
    rin_ref, rcot_ref, act_ref, gb_ref, ub_ref, rback_ref = refs[
        2 * count + 5 : 2 * count + 11
    ]
    weight_ref, gg_ref = refs[2 * count + 11 :]
    expert, part = pl.program_id(0), pl.program_id(1)
    tokens = x_refs[0].shape[0]
    slots = rin_ref.shape[1] // count

    def pick_of(block):
        places = lax.broadcasted_iota(jnp.int32, (slots, tokens), 0)
        return places == slot_ref[0, block : block + 1, :]

    def low(mask):
        return jnp.where(mask, 1.0, 0.0).astype(BF16)

    @pl.when(part == 0)
    def _():
        mine = base_ref[0] + expert
        for block in range(count):
            rows = pl.ds(block * slots, slots)
            pick = pick_of(block)
            pick_low = low(pick)
            x_block = x_refs[block][...]
            rin_ref[0, rows, :] = dot_f32(pick_low, x_block, ((1,), (0,))).astype(BF16)
            rcot_ref[0, rows, :] = dot_f32(
                pick_low, dy_refs[block][...], ((1,), (0,))
            ).astype(BF16)
            logits = dot_f32(router_ref[...], x_block, ((1,), (1,)))
            powers = jnp.exp(logits - jnp.max(logits, axis=0, keepdims=True))
            router = powers / jnp.sum(powers, axis=0, keepdims=True)
            which = lax.broadcasted_iota(jnp.int32, router.shape, 0)
            gate = jnp.sum(jnp.where(which == mine, router, 0.0), axis=0, keepdims=True)
            weight_ref[rows, :] = jnp.sum(
                jnp.where(pick, gate, 0.0), axis=1, keepdims=True
            )

    rows_in, rows_cot = rin_ref[0], rcot_ref[0]
    w_gate, w_up, w_back = wg_ref[0, 0, 0], wu_ref[0, 0, 0], wd_ref[0, 0]
    weight = weight_ref[...]
    pre_gate = dot_f32(rows_in, w_gate, ((1,), (0,)))
    pre_up = dot_f32(rows_in, w_up, ((1,), (0,)))
    cot_down = dot_f32(rows_cot, w_back, ((1,), (1,)))
    sigmoid = jax.nn.sigmoid(pre_gate)
    silu = pre_gate * sigmoid
    act = silu * pre_up
    share = act * cot_down
    folded = share[:, :128]
    for lane in range(128, share.shape[1], 128):
        folded = folded + share[:, lane : lane + 128]
    act_back = weight * cot_down
    act_ref[0] = (weight * act).astype(BF16)
    gb_ref[0] = (act_back * pre_up * (sigmoid + silu * (1.0 - sigmoid))).astype(BF16)
    ub_ref[0] = (act_back * silu).astype(BF16)

    @pl.when(part == 0)
    def _():
        gg_ref[...] = folded

    @pl.when(part > 0)
    def _():
        gg_ref[...] += folded

    @pl.when(part == pl.num_programs(1) - 1)
    def _():
        for block in range(count):
            rows = pl.ds(block * slots, slots)
            pick = pick_of(block)
            share = jnp.sum(gg_ref[rows, :], axis=1, keepdims=True)
            rback_ref[0, block : block + 1, :] = jnp.sum(
                jnp.where(pick, share, 0.0), axis=0, keepdims=True
            )


def weight_spec(shape, which=None):
    if which is None:
        return pl.BlockSpec((1, 1) + shape[2:], lambda e, j: (j, e, 0, 0))
    return pl.BlockSpec((1, 1, 1) + shape[3:], lambda e, j: (j, e, which, 0, 0))


def expert_group(base, x_blocks, dy_blocks, slot_of, router_rows, w_gate_up, w_down, slots, after):
    count = len(x_blocks)
    tokens, width = x_blocks[0].shape
    parts, experts, hidden = w_down.shape[:3]
    rows = count * slots

    def still(shape):
        return pl.BlockSpec(
            shape, lambda e, j: (0,) * len(shape), pipeline_mode=pl.Buffered(1)
        )

    def per_expert(*shape):
        return pl.BlockSpec((1,) + shape, lambda e, j: (e, 0, 0))

    part = pl.BlockSpec((1, rows, hidden), lambda e, j: (e, 0, j))
    wide = jax.ShapeDtypeStruct((experts, rows, width), BF16)
    deep = jax.ShapeDtypeStruct((experts, rows, parts * hidden), BF16)
    flops = 6 * rows * width * parts * hidden * experts
    return pl.pallas_call(
        functools.partial(expert_kernel, count, len(after)),
        grid=(experts, parts),
        in_specs=[pl.BlockSpec(memory_space=pltpu.SMEM)]
        + [pl.BlockSpec(memory_space=pl.ANY)] * len(after)
        + [still((tokens, width))] * (2 * count)
        + [
            per_expert(count, tokens),
            still(router_rows.shape),
            weight_spec(w_gate_up.shape, 0),
            weight_spec(w_gate_up.shape, 1),
            weight_spec(w_down.shape),
        ],
        out_specs=[
            per_expert(rows, width),
            per_expert(rows, width),
            part,
            part,
            part,
            per_expert(count, tokens),
        ],
        out_shape=[
            wide,
            wide,
            deep,
            deep,
            deep,
            jax.ShapeDtypeStruct((experts, count, tokens), F32),
        ],
        scratch_shapes=[
            pltpu.VMEM((rows, 1), F32),
            pltpu.VMEM((rows, 128), F32),
        ],
        compiler_params=pltpu.CompilerParams(vmem_limit_bytes=VMEM_BYTES),
        cost_estimate=pl.CostEstimate(
            flops=flops, bytes_accessed=3 * w_gate_up.size, transcendentals=rows * parts * hidden
        ),
        name="experts",
    )(base, *after, *x_blocks, *dy_blocks, slot_of, router_rows, w_gate_up, w_gate_up, w_down)


def combine_kernel(count, pairs, dim, slot_ref, *refs):
    lefts, weights = refs[:pairs], refs[pairs : 2 * pairs]
    terms_ref, acc_ref, sum_ref = refs[-3:]
    expert, part = pl.program_id(0), pl.program_id(1)
    tokens = terms_ref.shape[1]
    slots = acc_ref.shape[0] // count
    out = None
    for left, weight in zip(lefts, weights):
        matrix = weight[(0,) * (len(weight.shape) - 2)]
        product = dot_f32(left[0], matrix, ((1,), (dim,)))
        out = product if out is None else out + product

    @pl.when(part == 0)
    def _():
        acc_ref[...] = out

    @pl.when(part > 0)
    def _():
        acc_ref[...] += out

    @pl.when(part == pl.num_programs(1) - 1)
    def _():
        for block in range(count):
            places = lax.broadcasted_iota(jnp.int32, (slots, tokens), 0)
            pick = jnp.where(places == slot_ref[0, block : block + 1, :], 1.0, 0.0).astype(BF16)
            rows = acc_ref[pl.ds(block * slots, slots), :].astype(BF16)
            term = dot_f32(pick, rows, ((0,), (0,)))

            @pl.when(expert == 0)
            def _():
                sum_ref[block] = term

            @pl.when(expert > 0)
            def _():
                sum_ref[block] += term

            @pl.when(expert == pl.num_programs(0) - 1)
            def _():
                terms_ref[block] = sum_ref[block].astype(BF16)


def expert_combine(slot_of, lefts, weight, dim, after):
    experts, count, tokens = slot_of.shape
    parts = weight.shape[0]
    hidden, width = weight.shape[-2:] if dim == 0 else weight.shape[-1:-3:-1]
    rows = lefts[0].shape[1]
    pairs = len(lefts)
    which = range(pairs) if pairs > 1 else [None]
    return pl.pallas_call(
        functools.partial(combine_kernel, count, pairs, dim),
        grid=(experts, parts),
        in_specs=[pl.BlockSpec((1, count, tokens), lambda e, j: (e, 0, 0))]
        + [pl.BlockSpec((1, rows, hidden), lambda e, j: (e, 0, j))] * pairs
        + [weight_spec(weight.shape, place) for place in which]
        + [pl.BlockSpec(memory_space=pl.ANY)] * len(after),
        out_specs=pl.BlockSpec((count, tokens, width), lambda e, j: (0, 0, 0)),
        out_shape=jax.ShapeDtypeStruct((count, tokens, width), BF16),
        scratch_shapes=[
            pltpu.VMEM((rows, width), F32),
            pltpu.VMEM((count, tokens, width), F32),
        ],
        compiler_params=pltpu.CompilerParams(vmem_limit_bytes=VMEM_BYTES),
        cost_estimate=pl.CostEstimate(
            flops=2 * pairs * rows * width * parts * hidden * experts,
            bytes_accessed=2 * (weight.size + pairs * lefts[0].size + count * tokens * width),
            transcendentals=0,
        ),
        name="expert_combine",
    )(slot_of, *lefts, *[weight] * pairs, *after)


def grad_kernel(groups, *refs):
    total = None
    for left, right in zip(refs[:groups], refs[groups : 2 * groups]):
        part = dot_f32(left[0], right[0], ((0,), (0,)))
        total = part if total is None else total + part
    refs[-1][0, 0] = total.astype(BF16)


def expert_grad(lefts, rights, parts, after):
    experts = lefts[0].shape[0]
    hidden = min(lefts[0].shape[2], rights[0].shape[2]) // parts

    def spec(array, cut):
        width = hidden if cut else array.shape[2]
        return pl.BlockSpec(
            (1, array.shape[1], width), lambda e, j: (e, 0, j if cut else 0)
        )

    cut_left = lefts[0].shape[2] < rights[0].shape[2]
    shape = (
        hidden if cut_left else lefts[0].shape[2],
        rights[0].shape[2] if cut_left else hidden,
    )
    rows = sum(left.shape[1] for left in lefts)
    return pl.pallas_call(
        functools.partial(grad_kernel, len(lefts)),
        grid=(experts, parts),
        in_specs=[spec(left, cut_left) for left in lefts]
        + [spec(right, not cut_left) for right in rights]
        + [pl.BlockSpec(memory_space=pl.ANY)] * len(after),
        out_specs=pl.BlockSpec((1, 1) + shape, lambda e, j: (j, e, 0, 0)),
        out_shape=jax.ShapeDtypeStruct((parts, experts) + shape, BF16),
        compiler_params=pltpu.CompilerParams(vmem_limit_bytes=VMEM_BYTES),
        cost_estimate=pl.CostEstimate(
            flops=2 * rows * shape[0] * shape[1] * parts * experts,
            bytes_accessed=2 * experts * (parts * shape[0] * shape[1] + 3 * rows * shape[0]),
            transcendentals=0,
        ),
        name="expert_grad",
    )(*lefts, *rights, *after)


def on_device(
    tokens,
    out_grad,
    routes,
    segments,
    capacity,
    attn_gain,
    w_qkv,
    query_gain,
    key_gain,
    w_out,
    ffn_gain,
    w_router,
    w_gate_up,
    w_down,
):
    n_expert = lax.axis_size("expert")
    n_shard = lax.axis_size("shard")
    rows, width = tokens.shape
    size = width // HEADS
    heads = HEADS // n_shard
    local_width = heads * size
    length = segments.shape[0]
    expert_count = capacity.shape[0]
    local_experts = w_down.shape[0]
    slots = rows * routes.shape[1] // expert_count
    shard_index = lax.axis_index("shard")
    expert_index = lax.axis_index("expert")
    source, behind = ring_place(n_expert)
    part_rows = w_qkv.shape[0]
    slice_rows = part_rows // n_expert
    relative = jnp.bitwise_xor(shard_index, jnp.arange(n_shard, dtype=jnp.int32))

    packed = jnp.concatenate(
        [attn_gain, ffn_gain, query_gain, key_gain, w_router.reshape(-1)]
    )
    packed = lax.all_to_all(
        jnp.broadcast_to(packed[None], (n_shard, packed.shape[0])), "shard", 0, 0, tiled=True
    )
    cuts = [part_rows, 2 * part_rows, 2 * part_rows + size // n_shard]
    cuts.append(cuts[-1] + size // n_shard)
    gain_one = packed[:, : cuts[0]].reshape(1, width).astype(F32)
    gain_two = packed[:, cuts[0] : cuts[1]].reshape(1, width).astype(F32)
    gain_query = packed[:, cuts[1] : cuts[2]].reshape(1, size).astype(F32)
    gain_key = packed[:, cuts[2] : cuts[3]].reshape(1, size).astype(F32)
    full_router = packed[:, cuts[3] :].reshape(width, expert_count)
    router_rows = full_router.T

    own_slice = lax.dynamic_slice_in_dim(w_qkv, expert_index * slice_rows, slice_rows)
    own_slice = own_slice.reshape(slice_rows, 3, n_shard, local_width).transpose(2, 0, 1, 3)
    own_slice = lax.all_to_all(
        own_slice.reshape(n_shard, slice_rows, 3 * local_width), "shard", 0, 0, tiled=True
    )
    own_slice = own_slice.reshape(n_shard * slice_rows, 3 * local_width)

    ahead, back = ring_perms(n_expert)
    dy_first = (
        lax.ppermute(out_grad, "expert", ahead),
        lax.ppermute(out_grad, "expert", back),
    )
    w_blocks = ring_gather(tied(own_slice, dy_first), n_expert)
    w_local = jnp.zeros((n_shard, n_expert, slice_rows, 3 * local_width), BF16)
    for r in arrivals(n_expert):
        w_local = lax.dynamic_update_slice(
            w_local,
            w_blocks[r].reshape(n_shard, 1, slice_rows, 3 * local_width),
            (0, source[r], 0, 0),
        )
    w_local = w_local.reshape(width, 3 * local_width)

    token_parts = shard_gather(tied(tokens, own_slice))
    token_blocks = jnp.concatenate(token_parts, axis=0)

    routes_all = lax.all_to_all(
        jnp.broadcast_to(routes[None], (n_expert,) + routes.shape), "expert", 0, 0, tiled=True
    )[source]

    gate_up_full = lax.all_gather(w_gate_up, "shard")
    down_full = lax.all_gather(w_down, "shard")

    my_experts = expert_index * local_experts + jnp.arange(local_experts, dtype=jnp.int32)
    named = jnp.any(
        routes_all[None, :, :, :] == my_experts[:, None, None, None], axis=3
    )
    order = jnp.arange(rows, dtype=jnp.int32)
    before = (order[:, None] < order[None, :]).astype(BF16)
    earlier = jnp.einsum(
        "ebu,ut->ebt", named.astype(BF16), before, preferred_element_type=F32
    ).astype(jnp.int32)
    my_limits = lax.dynamic_slice_in_dim(capacity, expert_index * local_experts, local_experts)
    slot_of = jnp.where(named & (earlier < my_limits[:, None, None]), earlier, -1)

    position = (
        relative[:, None] * rows + jnp.arange(rows, dtype=jnp.int32)[None, :]
    ).reshape(-1).astype(F32)
    half_size = size // 2
    frequency = THETA ** (-(2.0 * jnp.arange(half_size, dtype=F32)) / size)
    angles = position[:, None] * frequency[None, :]
    cosines, sines = jnp.cos(angles), jnp.sin(angles)
    docs = segments.reshape(n_shard, rows)[relative].reshape(-1)
    tables = (
        jnp.concatenate([cosines, cosines], axis=1),
        jnp.concatenate([-sines, sines], axis=1),
        docs[:, None],
        docs[None, :],
        gain_query,
        gain_key,
    )

    token_float = token_blocks.astype(F32)
    scale_one = rms_scale(token_float)
    normed = (token_float * scale_one * gain_one).astype(BF16)
    qkv_pre = jnp.dot(normed, w_local, preferred_element_type=F32)
    mixed = attention(qkv_pre, tables, heads, size)
    dy_blocks = ring_rest(
        out_grad, dy_first, n_expert, {2: w_blocks[n_expert // 2], 3: mixed}
    )
    attended = jnp.dot(tied(mixed, dy_blocks[2]), w_out, preferred_element_type=F32).astype(BF16)
    own_tokens = tokens.astype(F32)
    hidden = own_tokens + shard_scatter(list(attended.reshape(n_shard, rows, width)))
    scale_two = rms_scale(hidden)
    ffn_low = (
        hidden * scale_two * gain_two
        + zero_of(dy_blocks[n_expert // 2 - 1], dy_blocks[n_expert // 2 + 1])
    ).astype(BF16)
    router = jax.nn.softmax(
        jnp.dot(ffn_low, full_router, preferred_element_type=F32), axis=-1
    )

    ffn_blocks = ring_gather(tied(ffn_low, dy_blocks[3]), n_expert, whole=False)
    groups = block_groups(n_expert)
    base = (expert_index * local_experts).reshape(1).astype(jnp.int32)
    results, slot_groups = [], []
    for group in groups:
        slots_g = jnp.stack([slot_of[:, r] for r in group], axis=1)
        if n_expert // 2 in group:
            ring_last(ffn_blocks, n_expert, [results[0][-1]] if results else ())
        slot_groups.append(slots_g)
        results.append(
            expert_group(
                base,
                [ffn_blocks[r] for r in group],
                [dy_blocks[r] for r in group],
                slot_groups[-1],
                router_rows,
                gate_up_full,
                down_full,
                slots,
                [results[-1][-1]] if results else [],
            )
        )
    rows_in, rows_cot, act, gate_back, up_back, router_terms = map(list, zip(*results))
    where_is = {r: (g, i) for g, group in enumerate(groups) for i, r in enumerate(group)}

    def picker(arrays):
        return lambda r: arrays[where_is[r][0]][where_is[r][1]]

    out_terms, terms = [None] * len(groups), [None] * len(groups)
    latest = router_terms[-1]
    last = len(groups) - 1
    out_hops = []

    def pick_out(r):
        g, place_in = where_is[r]
        if out_terms[g] is None:
            after = [out_terms[g + 1]] if g < last else [router_terms[-1]]
            after += out_hops[:1] if g == 0 else []
            out_terms[g] = expert_combine(slot_groups[g], [act[g]], down_full, 0, after)
        return out_terms[g][place_in]

    for g in range(last, 0, -1):
        pick_out(groups[g][0])
    out_sum, _ = ring_scatter(pick_out, n_expert, brought=out_hops)
    layer_out = (hidden + out_sum).astype(BF16)
    latest = out_terms[0]
    for g in range(last, -1, -1):
        latest = terms[g] = expert_combine(
            slot_groups[g],
            [gate_back[g], up_back[g]],
            gate_up_full,
            1,
            [latest] + (out_hops[1:2] if g == last - 1 else []),
        )
    back_hops = []
    ffn_back, _ = ring_scatter(picker(terms), n_expert, after=out_hops[2:3], brought=back_hops)
    back_to = jnp.stack(
        [router_terms[where_is[r][0]][:, where_is[r][1]] for r in range(n_expert)]
    )
    router_back = lax.all_to_all(
        back_to[behind], "expert", split_axis=0, concat_axis=0, tiled=True
    ).reshape(expert_count, rows).T

    gate_parts = expert_grad(rows_in, gate_back, n_shard, [latest] + out_hops[2:3])
    up_parts = expert_grad(rows_in, up_back, n_shard, [gate_parts] + back_hops[:1])
    down_parts = expert_grad(act, rows_cot, n_shard, [up_parts] + back_hops[1:2])
    ffn_back = ffn_back + zero_of(down_parts)

    logit_back = (
        router * (router_back - jnp.sum(router * router_back, axis=-1, keepdims=True))
    ).astype(BF16)
    router_grad = dot_f32(ffn_low, logit_back, ((0,), (0,)))
    ffn_back = ffn_back + dot_f32(logit_back, full_router, ((1,), (1,)))
    gain_two_part = jnp.sum(ffn_back * hidden * scale_two, axis=0)
    hidden_back = out_grad.astype(F32) + norm_back(ffn_back, hidden, scale_two, gain_two)

    hidden_low = hidden_back.astype(BF16)
    mix_parts = shard_gather(hidden_low)
    mix_back = jnp.concatenate(mix_parts, axis=0)

    gate_grads = shard_scatter(
        [
            lax.dynamic_index_in_dim(gate_parts, relative[r], 0, keepdims=False)
            for r in range(n_shard)
        ]
    )
    up_grads, down_grads = (
        lax.psum_scatter(
            parts.reshape((n_shard * local_experts,) + parts.shape[2:]),
            "shard",
            scatter_dimension=0,
            tiled=True,
        ).astype(F32)
        for parts in (up_parts, down_parts)
    )

    head_back = dot_f32(mix_back, w_out, ((1,), (1,))).astype(BF16)
    out_part = dot_f32(mixed, mix_back, ((0,), (0,))).astype(BF16)
    backs, head_gains, count = [], 0.0, heads // ATTENTION_PARTS
    for part in range(ATTENTION_PARTS):
        *back, gains = attention_back(
            qkv_pre, head_back, tables, heads, size, part * count, count
        )
        backs.append(back)
        head_gains = head_gains + gains
    qkv_back = jnp.concatenate([back[i] for i in range(3) for back in backs], axis=1)
    qkv_part = dot_f32(normed, qkv_back, ((0,), (0,))).astype(BF16)
    qkv_terms = qkv_part.reshape(n_shard, n_expert, slice_rows, 3 * local_width)
    qkv_mine, qkv_hops = ring_scatter(
        lambda r: lax.dynamic_index_in_dim(qkv_terms, source[r], 1, keepdims=False).reshape(
            n_shard * slice_rows, 3 * local_width
        ),
        n_expert,
    )
    normed_back = dot_f32(held(qkv_back, qkv_hops[1]), w_local, ((1,), (1,)))
    gain_one_part = jnp.sum(normed_back * token_float * scale_one, axis=0)
    own_back = shard_scatter(
        list(normed_back.astype(BF16).reshape(n_shard, rows, width))
    )
    tokens_grad = hidden_back + norm_back(own_back, own_tokens, scale_one[:rows], gain_one)

    def placed_blocks(blocks):
        total = jnp.zeros((n_expert * blocks[0].shape[0], blocks[0].shape[1]), F32)
        for r in arrivals(n_expert):
            total = lax.dynamic_update_slice(
                total, blocks[r].astype(F32), (source[r] * blocks[r].shape[0], 0)
            )
        return total

    out_total = lax.psum(out_part, "expert").astype(F32)
    qkv_mine = lax.all_to_all(
        qkv_mine.astype(BF16), "shard", split_axis=0, concat_axis=0, tiled=True
    )
    qkv_mine = (
        qkv_mine.reshape(n_shard, slice_rows, 3, local_width)
        .transpose(1, 2, 0, 3)
        .reshape(slice_rows, 3 * width)
    )
    qkv_total = placed_blocks(ring_gather(qkv_mine, n_expert))

    small = jnp.concatenate(
        [
            gain_one_part.reshape(n_shard, -1),
            gain_two_part.reshape(n_shard, -1),
            head_gains[0].reshape(n_shard, -1),
            head_gains[1].reshape(n_shard, -1),
            router_grad.reshape(n_shard, -1),
        ],
        axis=1,
    )
    small = held(small, qkv_hops[1])
    small = lax.all_to_all(small, "shard", split_axis=0, concat_axis=0, tiled=True)
    small = tree_sum(jnp.sum(small, axis=0).reshape(1, -1), "expert")[0]
    gate_up_grad = jnp.stack([gate_grads, up_grads], axis=1)
    return (
        layer_out,
        tokens_grad,
        small[: cuts[0]],
        qkv_total,
        small[cuts[1] : cuts[2]],
        small[cuts[2] : cuts[3]],
        out_total,
        small[cuts[0] : cuts[1]],
        small[cuts[3] :].reshape(part_rows, expert_count),
        gate_up_grad,
        down_grads,
    )


def solution(mesh):
    placed = (
        P(("expert", "shard"), None),
        P(("expert", "shard"), None),
        P(("expert", "shard"), None),
        P("expert"),
        P(),
        P("shard"),
        P("shard", None),
        P("shard"),
        P("shard"),
        P("shard", None),
        P("shard"),
        P("shard", None),
        P("expert", None, None, "shard"),
        P("expert", "shard", None),
    )
    return jax.shard_map(
        on_device,
        mesh=mesh,
        in_specs=placed,
        out_specs=(
            P(("expert", "shard"), None),
            P(("expert", "shard"), None),
            P("shard"),
            P("shard", None),
            P("shard"),
            P("shard"),
            P("shard", None),
            P("shard"),
            P("shard", None),
            P("expert", None, None, "shard"),
            P("expert", "shard", None),
        ),
        check_vma=False,
    )
```
